32 devices in a mesh: rep: 16 (over z, x, core), exp: 2 (over y).
Axes of the slice: x: 2, y: 2, z: 4, core: 2. Of those that a mesh axis runs over, the one named last changes fastest.
Arguments:
- hidden_states: bfloat16 [8192, 384], P(('rep', 'exp')), may hold values from -6 to 6
- expert_ids: int32 [8192, 2], P(('rep', 'exp')), may hold values from 0 to 7, all different within a row; in each aligned block of 256 rows (0 to 255, 256 to 511, ...) at most 96 rows name the same one
- router_weight: bfloat16 [384, 8], replicated, may hold values from -0.3125 to 0.3125
- up_weight: bfloat16 [8, 384, 2048], P('exp'), may hold values from -0.3125 to 0.3125
- down_weight: bfloat16 [8, 2048, 384], P('exp'), may hold values from -0.125 to 0.125
- projection: bfloat16 [384, 128], replicated, may hold values from -0.3125 to 0.3125
- teacher_scores: float32 [32, 32, 224], P(('rep', 'exp')), may hold values from -8 to 8
- query_lengths: int32 [32], P(('rep', 'exp')), may hold values from 8 to 32
- passage_lengths: int32 [32], P(('rep', 'exp')), may hold values from 56 to 224
Outputs:
- input_grad: bfloat16 [8192, 384], P(('rep', 'exp'))
- down_grad: float32 [8, 2048, 384], P('exp', 'rep')
- pair_kl: float32 [32], P(('rep', 'exp'))
The draws below stay inside these ranges and needn't reach their ends.
Inputs may be any that keep to these rules, and one draw needn't show every extreme that they name: `expert_ids`: each row names 2 different experts. In the 256 rows of one device no expert is named more than 96 times, and in every draw some device names some expert exactly 96 times.
All inputs are finite; a program needn't handle non-finite values.
Results may differ from the reference program's by a relative error of at most 0.0086.
Values may be sent and summed in bfloat16 or wider, within the bound.
A program may use at most 64 MiB of HBM per device.

```python
import math
import jax
import jax.numpy as jnp
import numpy as np
from jax import lax

D = 384
FF = 2048
E = 8
TOP = 2
VEC = 128
LQ = 32
LP = 224
SEQ = 256
TOK_DEV = 256
CAP = 96
PAIRS = 32
TOKENS = 8192


def place_ends(entries, stream_key, low, high):
    index_at = [jax.random.randint(jax.random.fold_in(stream_key, axis), (), 0, length) for axis, length in enumerate(entries.shape)]
    widest = entries.shape.index(max(entries.shape))
    neighbour = index_at[:widest] + [(index_at[widest] + 1) % entries.shape[widest]] + index_at[widest + 1:]
    return entries.at[tuple(index_at)].set(low).at[tuple(neighbour)].set(high)


def steps_of(key, extent, split, smallest, high):
    def one(position, blocks):
        draws = jax.random.uniform(jax.random.fold_in(jax.random.fold_in(key, 6), position), (blocks,), jnp.float32, smallest / len(split), high / len(split))
        return jnp.repeat(jnp.exp(draws), extent[position] // blocks).reshape((-1,) + (1,) * (len(extent) - position - 1))

    loudness = one(*split[0])
    for cut in split[1:]:
        loudness = loudness * one(*cut)
    return loudness


def assign_block(stream_key, own, number, rows, number_of, top, reach, skew):
    order = jax.random.permutation(stream_key, number_of)
    crowded, ordinary = shares(number_of, rows * top, reach, skew, True), shares(number_of, rows * top, reach, skew, False)
    places = jnp.arange(number_of)

    def named(lengths, offset_by):
        used = int((lengths > 0).sum())
        fixed = max(1, used // 4)
        shifted = fixed + (places - fixed + offset_by * (used - fixed)) % max(1, number_of - fixed)
        return jnp.zeros((number_of,), jnp.int32).at[order[jnp.where(places < fixed, places, shifted)]].set(jnp.asarray(lengths, jnp.int32))

    lengths = jnp.where(number % 4 == 0, named(crowded, number // 4), named(ordinary, number - number // 4 - 1))
    mixed = jax.random.permutation(jax.random.fold_in(own, 3), number_of)
    source_of, taker = mixed[0:number_of // 2 * 2:2], mixed[1:number_of // 2 * 2:2]
    margin = jnp.minimum(lengths[source_of] - 1, reach - lengths[taker]) // 2
    margin = jnp.where((source_of == order[0]) | (taker == order[0]) | (lengths[taker] == 0), 0, jnp.maximum(margin, 0))
    shifted = jax.random.randint(jax.random.fold_in(own, 4), (number_of // 2,), 0, 1 << 20) % (margin + 1)
    lengths = lengths.at[source_of].add(-shifted).at[taker].add(shifted)
    labels = jnp.searchsorted(jnp.cumsum(lengths), jnp.arange(rows * top), side="right").astype(jnp.int32)
    grid = labels.reshape(top, rows).T
    grid = grid[jax.random.permutation(jax.random.fold_in(own, 1), rows)]
    offset_by = jax.random.randint(jax.random.fold_in(own, 2), (rows, 1), 0, top)
    return jnp.take_along_axis(grid, (jnp.arange(top)[None, :] + offset_by) % top, axis=1)


def shares(amount, total, limit, slope, full):
    loads = [(1 << 20) // math.isqrt(standing ** slope) + 1 for standing in range(1, amount + 1)]
    largest = limit if full else min(limit, max(-(-total // amount), total * loads[0] // sum(loads)))
    least = 1 if total - largest >= amount - 1 else 0
    holding, spare = [largest] + [least] * (amount - 1), total - largest - least * (amount - 1)
    while spare > 0:
        candidates = [i for i in range(1, amount) if holding[i] < largest] or [i for i in range(1, amount) if holding[i] < limit]
        pool, budget = sum([loads[i] for i in candidates]), spare
        for i in candidates:
            addition = min(limit - holding[i], max(1, budget * loads[i] // pool), spare)
            holding[i] = holding[i] + addition
            spare = spare - addition
    return np.array(holding)


def bell_draw(rng, extent, deviation, reach, cuts=(), kind=jnp.bfloat16):
    result = deviation * jax.random.normal(rng, extent, jnp.float32)
    if cuts:
        result = result * steps_of(rng, extent, cuts, -0.22, 0.18)
    return jnp.clip(result, -reach, reach).astype(kind)


def setup_inputs(seed: int = 0) -> dict:
    arg_keys = jax.random.split(jax.random.key(seed), 10)
    hidden_states = bell_draw(arg_keys[0], (TOKENS, D), 1.0, 6.0, ((0, 32),))
    expert_ids_keys = jax.random.split(jax.random.fold_in(arg_keys[1], 1), TOKENS // TOK_DEV)
    expert_ids_turns = jax.random.permutation(jax.random.fold_in(arg_keys[1], 3), TOKENS // TOK_DEV)
    expert_ids = jax.vmap(lambda own, number: assign_block(jax.random.fold_in(arg_keys[1], 2), own, number, TOK_DEV, E, TOP, CAP, 2))(expert_ids_keys, expert_ids_turns).reshape((TOKENS, TOP))
    router_weight = bell_draw(arg_keys[2], (D, E), D ** -0.5, 0.3125)
    up_weight = bell_draw(arg_keys[3], (E, D, FF), D ** -0.5, 0.3125, ((0, 2),))
    down_weight = bell_draw(arg_keys[4], (E, FF, D), FF ** -0.5, 0.125, ((0, 2),))
    projection = bell_draw(arg_keys[5], (D, VEC), D ** -0.5, 0.3125)
    teacher_scores = jnp.clip(jax.random.uniform(arg_keys[6], (PAIRS, LQ, LP), jnp.float32, -8.0, 8.0) * steps_of(arg_keys[6], (PAIRS, LQ, LP), ((0, 32),), -0.4, 0.0), -8.0, 8.0)
    query_lengths = place_ends(jax.random.randint(arg_keys[7], (PAIRS,), LQ // 4, LQ + 1), jax.random.fold_in(arg_keys[7], 1), LQ // 4, LQ).astype(jnp.int32)
    passage_lengths = place_ends(jax.random.randint(arg_keys[8], (PAIRS,), LP // 4, LP + 1), jax.random.fold_in(arg_keys[8], 1), LP // 4, LP).astype(jnp.int32)
    return {"hidden_states": hidden_states, "expert_ids": expert_ids, "router_weight": router_weight, "up_weight": up_weight, "down_weight": down_weight, "projection": projection, "teacher_scores": teacher_scores, "query_lengths": query_lengths, "passage_lengths": passage_lengths}


score_scale = 20.0
norm_eps = 1e-06
sqrt_half = 0.7071067811865476
density_scale = 0.3989422804014327

def gelu_value(preact):
    return 0.5 * preact * (1.0 + lax.erf(preact * sqrt_half))

def gelu_slope(preact):
    return 0.5 * (1.0 + lax.erf(preact * sqrt_half)) + preact * jnp.exp(-0.5 * preact * preact) * density_scale

def distill(vectors, teacher_scores, query_lengths, passage_lengths):
    queries = vectors[:, :LQ]
    passages = vectors[:, LQ:]
    scores = score_scale * jnp.einsum('pqv,pkv->pqk', queries, passages, precision=lax.Precision.HIGHEST)
    query_mask = (jnp.arange(LQ, dtype=jnp.int32)[None, :] < query_lengths[:, None]).astype(jnp.float32)
    passage_mask = (jnp.arange(LP, dtype=jnp.int32)[None, :] < passage_lengths[:, None]).astype(jnp.float32)
    student_exp = jnp.exp(scores) * passage_mask[:, None, :]
    student_total = lax.optimization_barrier(jnp.sum(student_exp, axis=-1, keepdims=True))
    student = student_exp / student_total
    log_student = scores - jnp.log(student_total)
    teacher_exp = jnp.exp(teacher_scores) * passage_mask[:, None, :]
    teacher_total = lax.optimization_barrier(jnp.sum(teacher_exp, axis=-1, keepdims=True))
    teacher = teacher_exp / teacher_total
    log_teacher = teacher_scores - jnp.log(teacher_total)
    per_query = lax.optimization_barrier(jnp.sum(teacher * (log_teacher - log_student), axis=-1))
    pair_kl = lax.optimization_barrier(jnp.sum(per_query * query_mask, axis=-1))
    score_grad = (student - teacher) * query_mask[:, :, None]
    query_grad = score_scale * jnp.einsum('pqk,pkv->pqv', score_grad, passages, precision=lax.Precision.HIGHEST)
    passage_grad = score_scale * jnp.einsum('pqk,pqv->pkv', score_grad, queries, precision=lax.Precision.HIGHEST)
    return (pair_kl, jnp.concatenate([query_grad, passage_grad], axis=1))

def route_targets(block_ids):
    onehot = (block_ids[..., None] == jnp.arange(E, dtype=jnp.int32)).astype(jnp.int32)
    earlier = jnp.cumsum(onehot, axis=1) - onehot
    slots = lax.optimization_barrier(jnp.sum(earlier * onehot, axis=-1))
    return (block_ids * CAP + slots).astype(jnp.int32)

def group_blocks(expert_rows):
    groups = expert_rows.shape[0]
    per_block = 16 if groups % 16 == 0 else 1
    return expert_rows.reshape(groups // per_block, per_block * CAP, D)

def expert_forward(operands):
    weight_up, weight_down, expert_rows = operands

    def one_block(block_rows):
        preact = jnp.dot(block_rows, weight_up, preferred_element_type=jnp.float32)
        hidden = gelu_value(preact).astype(jnp.bfloat16)
        return jnp.dot(hidden, weight_down, preferred_element_type=jnp.float32).astype(jnp.bfloat16)
    outputs = lax.map(one_block, group_blocks(expert_rows))
    return outputs.reshape(expert_rows.shape)

def expert_backward(operands):
    weight_up, weight_down, expert_rows, expert_grads = operands

    def one_block(total, pieces):
        block_rows, block_grads = pieces
        preact = jnp.dot(block_rows, weight_up, preferred_element_type=jnp.float32)
        hidden = gelu_value(preact).astype(jnp.bfloat16)
        total = total + jnp.dot(hidden.T, block_grads, preferred_element_type=jnp.float32)
        hidden_grad = jnp.dot(block_grads, weight_down.T, preferred_element_type=jnp.float32)
        pre_grad = (hidden_grad * gelu_slope(preact)).astype(jnp.bfloat16)
        row_grad = jnp.dot(pre_grad, weight_up.T, preferred_element_type=jnp.float32).astype(jnp.bfloat16)
        return (total, row_grad)
    initial = jnp.zeros((FF, D), jnp.float32)
    total, row_grads = lax.scan(one_block, initial, (group_blocks(expert_rows), group_blocks(expert_grads)))
    return (total, row_grads.reshape(expert_rows.shape))

def reference(hidden_states, expert_ids, router_weight, up_weight, down_weight, projection, teacher_scores, query_lengths, passage_lengths):
    groups = TOKENS // TOK_DEV
    route_count = TOK_DEV * TOP
    logits = jnp.dot(hidden_states, router_weight, preferred_element_type=jnp.float32)
    choose = (expert_ids[..., None] == jnp.arange(E, dtype=jnp.int32)).astype(jnp.float32)
    picked = lax.optimization_barrier(jnp.sum(logits[:, None, :] * choose, axis=-1))
    first_gate = jax.nn.sigmoid(picked[:, 0] - picked[:, 1])
    gate_values = jnp.stack([first_gate, 1.0 - first_gate], axis=1)
    targets = route_targets(expert_ids.reshape(groups, route_count))
    group_index = jnp.arange(groups, dtype=jnp.int32)[:, None]
    routed = jnp.repeat(hidden_states, TOP, axis=0).reshape(groups, route_count, D)
    buffers = jnp.zeros((groups, E * CAP, D), hidden_states.dtype).at[group_index, targets].set(routed)
    by_expert = buffers.reshape(groups, E, CAP, D).transpose(1, 0, 2, 3)
    outputs = lax.map(expert_forward, (up_weight, down_weight, by_expert))
    outputs_flat = outputs.transpose(1, 0, 2, 3).reshape(groups, E * CAP, D)
    picked_out = jnp.take_along_axis(outputs_flat, targets[..., None], axis=1).reshape(TOKENS, TOP, D)
    mixed_rows = (hidden_states.astype(jnp.float32) + lax.optimization_barrier(jnp.sum(gate_values[:, :, None] * picked_out.astype(jnp.float32), axis=1))).astype(jnp.bfloat16)
    projected = jnp.dot(mixed_rows, projection, preferred_element_type=jnp.float32)
    vec_norm = jnp.sqrt(lax.optimization_barrier(jnp.sum(projected * projected, axis=-1, keepdims=True)) + norm_eps)
    vectors = projected / vec_norm
    pair_kl, vector_grad = distill(vectors.reshape(PAIRS, SEQ, VEC), teacher_scores, query_lengths, passage_lengths)
    vector_grad = vector_grad.reshape(TOKENS, VEC)
    radial = lax.optimization_barrier(jnp.sum(vectors * vector_grad, axis=-1, keepdims=True))
    projected_grad = ((vector_grad - vectors * radial) / vec_norm).astype(jnp.bfloat16)
    mixed_grad = jnp.dot(projected_grad, projection.T, preferred_element_type=jnp.float32)
    out_grad = (gate_values[:, :, None] * mixed_grad[:, None, :]).astype(jnp.bfloat16)
    gate_grad = lax.optimization_barrier(jnp.sum(mixed_grad[:, None, :] * picked_out.astype(jnp.float32), axis=-1))
    spread = (gate_grad[:, 0] - gate_grad[:, 1]) * gate_values[:, 0] * gate_values[:, 1]
    logit_grad = spread[:, None] * (choose[:, 0] - choose[:, 1])
    router_part = jnp.dot(logit_grad, router_weight.astype(jnp.float32).T, precision=lax.Precision.HIGHEST)
    grad_buffers = jnp.zeros((groups, E * CAP, D), out_grad.dtype).at[group_index, targets].set(out_grad.reshape(groups, route_count, D))
    grad_by_expert = grad_buffers.reshape(groups, E, CAP, D).transpose(1, 0, 2, 3)
    down_grad, returned = lax.map(expert_backward, (up_weight, down_weight, by_expert, grad_by_expert))
    returned_flat = returned.transpose(1, 0, 2, 3).reshape(groups, E * CAP, D)
    route_grad = jnp.take_along_axis(returned_flat, targets[..., None], axis=1).reshape(TOKENS, TOP, D)
    input_grad = (mixed_grad + lax.optimization_barrier(jnp.sum(route_grad.astype(jnp.float32), axis=1)) + router_part).astype(jnp.bfloat16)
    return (input_grad, down_grad, pair_kl)
```

```python
import jax
import jax.numpy as jnp
from jax import lax
from jax.sharding import PartitionSpec as P

E = 8
LQ = 32
LP = 224
CAP = 96


score_scale = 20.0
norm_eps = 1e-06
sqrt_half = 0.7071067811865476
density_scale = 0.3989422804014327


def gelu_value(preact):
    return 0.5 * preact * (1.0 + lax.erf(preact * sqrt_half))


def gelu_slope(preact):
    return (
        0.5 * (1.0 + lax.erf(preact * sqrt_half))
        + preact * jnp.exp(-0.5 * preact * preact) * density_scale
    )


def distill(vectors, teacher_scores, query_lengths, passage_lengths):
    queries = vectors[:, :LQ]
    passages = vectors[:, LQ:]
    scores = score_scale * jnp.einsum(
        "pqv,pkv->pqk", queries, passages, precision=lax.Precision.HIGHEST
    )
    query_mask = (jnp.arange(LQ, dtype=jnp.int32)[None, :] < query_lengths[:, None]).astype(
        jnp.float32
    )
    passage_mask = (jnp.arange(LP, dtype=jnp.int32)[None, :] < passage_lengths[:, None]).astype(
        jnp.float32
    )
    student_exp = jnp.exp(scores) * passage_mask[:, None, :]
    student_total = jnp.sum(student_exp, axis=-1, keepdims=True)
    student = student_exp / student_total
    log_student = scores - jnp.log(student_total)
    teacher_exp = jnp.exp(teacher_scores) * passage_mask[:, None, :]
    teacher_total = jnp.sum(teacher_exp, axis=-1, keepdims=True)
    teacher = teacher_exp / teacher_total
    log_teacher = teacher_scores - jnp.log(teacher_total)
    per_query = jnp.sum(teacher * (log_teacher - log_student), axis=-1)
    pair_kl = jnp.sum(per_query * query_mask, axis=-1)
    score_grad = (student - teacher) * query_mask[:, :, None]
    query_grad = score_scale * jnp.einsum(
        "pqk,pkv->pqv", score_grad, passages, precision=lax.Precision.HIGHEST
    )
    passage_grad = score_scale * jnp.einsum(
        "pqk,pqv->pkv", score_grad, queries, precision=lax.Precision.HIGHEST
    )
    return (pair_kl, jnp.concatenate([query_grad, passage_grad], axis=1))


def fetch(block, shift):
    size = lax.axis_size("exp")
    return lax.ppermute(block, "exp", [(i, (i - shift) % size) for i in range(size)])


def give_back(block, shift):
    size = lax.axis_size("exp")
    return lax.ppermute(block, "exp", [(i, (i + shift) % size) for i in range(size)])


def spread_out(block):
    size = lax.axis_size("exp")
    return jnp.stack([block] + [fetch(block, shift) for shift in range(1, size)])


def bring_home(parts):
    total = parts[0]
    for shift in range(1, parts.shape[0]):
        total = total + give_back(parts[shift].astype(jnp.bfloat16), shift).astype(jnp.float32)
    return total


def halving_orders(bits, experts):
    near = list(range(bits))
    late = [0] + list(range(2, bits)) + [1] if bits > 2 else near
    return [late if expert % 4 == 3 else near for expert in range(experts)]


def weight_grad(hidden, gated, projection, gate_rows):
    size = lax.axis_size("rep")
    bits = size.bit_length() - 1
    experts, _, units = hidden.shape
    width = gated.shape[-1]
    share = units // size
    index = lax.axis_index("rep")
    product = jnp.einsum(
        "erf,erv->efv", hidden, gated, preferred_element_type=jnp.float32
    ).astype(jnp.bfloat16)

    def swap(block, bit):
        return lax.ppermute(block, "rep", [(i, i ^ (1 << bit)) for i in range(size)])

    orders = halving_orders(bits, experts)
    left = [list(range(bits - 1, -1, -1)) for _ in range(experts)]
    held = [[product[e]] for e in range(experts)]
    for step in range(bits):
        sent = []
        for e in range(experts):
            bit = orders[e][step]
            axis = left[e].index(bit)
            shape = (2,) * len(left[e]) + (share, width)
            here = (index >> bit) % 2

            def half(side):
                total = None
                for term in held[e]:
                    piece = lax.dynamic_index_in_dim(
                        term.reshape(shape), side, axis=axis, keepdims=False
                    ).astype(jnp.float32)
                    total = piece if total is None else total + piece
                return total

            sent.append(half(1 - here).astype(jnp.bfloat16))
            held[e] = [half(here)]
            left[e].remove(bit)
        for e in range(experts):
            held[e].append(swap(sent[e], orders[e][step]))
        if step == min(1, bits - 1):
            held[-1], gate_rows = lax.optimization_barrier((held[-1], gate_rows))
    shares = [
        sum(term.astype(jnp.float32).reshape(share, width) for term in held[e])
        for e in range(experts)
    ]
    factor = jnp.stack(shares)
    grad = jnp.einsum(
        "efv,dv->efd",
        factor,
        projection.astype(jnp.float32),
        precision=lax.Precision.HIGHEST,
    )
    return grad, gate_rows


def local(
    hidden_states,
    expert_ids,
    router_weight,
    up_weight,
    down_weight,
    projection,
    teacher_scores,
    query_lengths,
    passage_lengths,
):
    tok_rows, width = hidden_states.shape
    here = up_weight.shape[0]
    first = lax.axis_index("exp") * here
    rows = spread_out(hidden_states)
    ids = spread_out(expert_ids.T)
    blocks = rows.shape[0]
    names = jnp.arange(E, dtype=jnp.int32)[None, :, None]
    is_first = (ids[:, :1] == names).astype(jnp.float32)
    is_second = (ids[:, 1:] == names).astype(jnp.float32)
    logits = jnp.einsum("de,ntd->net", router_weight, rows, preferred_element_type=jnp.float32)
    side = is_first - is_second
    first_gate = jax.nn.sigmoid(jnp.sum(logits * side, axis=1, keepdims=True))
    second_gate = 1.0 - first_gate
    named = is_first + is_second
    before = jnp.arange(tok_rows)[:, None] < jnp.arange(tok_rows)[None, :]
    slots = jnp.einsum(
        "net,tu->neu",
        named.astype(jnp.bfloat16),
        before.astype(jnp.bfloat16),
        preferred_element_type=jnp.float32,
    ).astype(jnp.int32)
    slots = jnp.where(named > 0, slots, -1)
    mine = lambda value: lax.dynamic_slice_in_dim(value, first, here, axis=1)
    slots_here = mine(slots)
    gates_here = mine(is_first * first_gate + is_second * second_gate)
    side_here = mine(side)
    hit = slots_here[:, :, None, :] == jnp.arange(CAP, dtype=jnp.int32)[None, None, :, None]
    pick = hit.astype(jnp.bfloat16)
    row_gate = jnp.sum(jnp.where(hit, gates_here[:, :, None, :], 0.0), axis=-1)
    row_gate = row_gate.transpose(1, 0, 2).reshape(here, blocks * CAP, 1)

    def to_slots(tokens):
        picked = jnp.einsum("nect,ntd->encd", pick, tokens, preferred_element_type=jnp.float32)
        return picked.astype(jnp.bfloat16).reshape(here, blocks * CAP, -1)

    def to_tokens(slot_rows):
        return jnp.einsum(
            "nect,encd->ntd",
            pick,
            slot_rows.reshape(here, blocks, CAP, width),
            preferred_element_type=jnp.float32,
        )

    expert_rows = to_slots(rows)
    preact = jnp.einsum(
        "erd,edf->erf", expert_rows, up_weight, preferred_element_type=jnp.float32
    )
    hidden = gelu_value(preact).astype(jnp.bfloat16)
    out = jnp.einsum("erf,efd->erd", hidden, down_weight, preferred_element_type=jnp.float32)
    mixed = bring_home(to_tokens((row_gate * out).astype(jnp.bfloat16)))
    mixed_rows = (hidden_states.astype(jnp.float32) + mixed).astype(jnp.bfloat16)
    projected = jnp.dot(mixed_rows, projection, preferred_element_type=jnp.float32)
    vec_norm = jnp.sqrt(jnp.sum(projected * projected, axis=-1, keepdims=True) + norm_eps)
    vectors = projected / vec_norm
    pairs_here = teacher_scores.shape[0]
    pair_kl, vector_grad = distill(
        vectors.reshape(pairs_here, -1, projected.shape[1]),
        teacher_scores,
        query_lengths,
        passage_lengths,
    )
    vector_grad = vector_grad.reshape(tok_rows, -1)
    radial = jnp.sum(vectors * vector_grad, axis=-1, keepdims=True)
    projected_grad = ((vector_grad - vectors * radial) / vec_norm).astype(jnp.bfloat16)
    mixed_grad = jnp.dot(projected_grad, projection.T, preferred_element_type=jnp.float32)
    pg_rows = to_slots(spread_out(projected_grad))
    grad_rows = jnp.einsum(
        "erv,dv->erd", pg_rows, projection, preferred_element_type=jnp.float32
    )
    out_grad = (row_gate * grad_rows).astype(jnp.bfloat16)
    gated = (row_gate * pg_rows.astype(jnp.float32)).astype(jnp.bfloat16)
    down_grad, out_grad = weight_grad(hidden, gated, projection, out_grad)
    gate_grad = jnp.sum(grad_rows * out, axis=-1).reshape(here, blocks, CAP).transpose(1, 0, 2)
    hit_grad = jnp.sum(jnp.where(hit, gate_grad[..., None], 0.0), axis=2)
    spread = jnp.sum(hit_grad * side_here, axis=1, keepdims=True) * first_gate * second_gate
    router_part = jnp.einsum(
        "net,de->ntd",
        spread * side,
        router_weight.astype(jnp.float32),
        precision=lax.Precision.HIGHEST,
    )
    hidden_grad = jnp.einsum(
        "erd,efd->erf", out_grad, down_weight, preferred_element_type=jnp.float32
    )
    pre_grad = (hidden_grad * gelu_slope(preact)).astype(jnp.bfloat16)
    row_grad = jnp.einsum(
        "erf,edf->erd", pre_grad, up_weight, preferred_element_type=jnp.float32
    ).astype(jnp.bfloat16)
    input_grad = (mixed_grad + bring_home(to_tokens(row_grad) + router_part)).astype(jnp.bfloat16)
    return (input_grad, down_grad, pair_kl)


def solution(mesh):
    placed = (
        P(("rep", "exp"), None),
        P(("rep", "exp"), None),
        P(),
        P("exp", None, None),
        P("exp", None, None),
        P(),
        P(("rep", "exp"), None, None),
        P(("rep", "exp")),
        P(("rep", "exp")),
    )
    return jax.shard_map(
        local,
        mesh=mesh,
        in_specs=placed,
        out_specs=(P(("rep", "exp"), None), P("exp", "rep", None), P(("rep", "exp"))),
        check_vma=False,
    )
```

```python
import jax
import jax.numpy as jnp
from jax import lax
from jax.experimental import pallas as pl
from jax.experimental.pallas import tpu as pltpu
from jax.sharding import PartitionSpec as P

E = 8
LQ = 32
LP = 224
CAP = 96


score_scale = 20.0
norm_eps = 1e-06
sqrt_half = 0.7071067811865476
density_scale = 0.3989422804014327


def gelu_value(preact):
    return 0.5 * preact * (1.0 + lax.erf(preact * sqrt_half))


def gelu_slope(preact):
    return (
        0.5 * (1.0 + lax.erf(preact * sqrt_half))
        + preact * jnp.exp(-0.5 * preact * preact) * density_scale
    )


def distill(vectors, teacher_scores, query_lengths, passage_lengths):
    queries = vectors[:, :LQ]
    passages = vectors[:, LQ:]
    scores = score_scale * jnp.einsum(
        "pqv,pkv->pqk", queries, passages, precision=lax.Precision.HIGHEST
    )
    query_mask = (jnp.arange(LQ, dtype=jnp.int32)[None, :] < query_lengths[:, None]).astype(
        jnp.float32
    )
    passage_mask = (jnp.arange(LP, dtype=jnp.int32)[None, :] < passage_lengths[:, None]).astype(
        jnp.float32
    )
    student_exp = jnp.exp(scores) * passage_mask[:, None, :]
    student_total = jnp.sum(student_exp, axis=-1, keepdims=True)
    student = student_exp / student_total
    log_student = scores - jnp.log(student_total)
    teacher_exp = jnp.exp(teacher_scores) * passage_mask[:, None, :]
    teacher_total = jnp.sum(teacher_exp, axis=-1, keepdims=True)
    teacher = teacher_exp / teacher_total
    log_teacher = teacher_scores - jnp.log(teacher_total)
    per_query = jnp.sum(teacher * (log_teacher - log_student), axis=-1)
    pair_kl = jnp.sum(per_query * query_mask, axis=-1)
    score_grad = (student - teacher) * query_mask[:, :, None]
    query_grad = score_scale * jnp.einsum(
        "pqk,pkv->pqv", score_grad, passages, precision=lax.Precision.HIGHEST
    )
    passage_grad = score_scale * jnp.einsum(
        "pqk,pqv->pkv", score_grad, queries, precision=lax.Precision.HIGHEST
    )
    return (pair_kl, jnp.concatenate([query_grad, passage_grad], axis=1))


def fetch(block, shift):
    size = lax.axis_size("exp")
    return lax.ppermute(block, "exp", [(i, (i - shift) % size) for i in range(size)])


def give_back(block, shift):
    size = lax.axis_size("exp")
    return lax.ppermute(block, "exp", [(i, (i + shift) % size) for i in range(size)])


def spread_out(block):
    size = lax.axis_size("exp")
    return jnp.stack([block] + [fetch(block, shift) for shift in range(1, size)])


def bring_home(parts):
    total = parts[0]
    for shift in range(1, parts.shape[0]):
        total = total + give_back(parts[shift].astype(jnp.bfloat16), shift).astype(jnp.float32)
    return total


def halving_orders(bits, experts):
    near = list(range(bits))
    late = [0] + list(range(2, bits)) + [1] if bits > 2 else near
    return [late if expert % 4 == 3 else near for expert in range(experts)]


def weight_grad(hidden, gated, projection, gate_rows):
    size = lax.axis_size("rep")
    bits = size.bit_length() - 1
    experts, _, units = hidden.shape
    width = gated.shape[-1]
    share = units // size
    index = lax.axis_index("rep")
    product = jnp.einsum(
        "erf,erv->efv", hidden, gated, preferred_element_type=jnp.float32
    ).astype(jnp.bfloat16)

    def swap(block, bit):
        return lax.ppermute(block, "rep", [(i, i ^ (1 << bit)) for i in range(size)])

    orders = halving_orders(bits, experts)
    left = [list(range(bits - 1, -1, -1)) for _ in range(experts)]
    held = [[product[e]] for e in range(experts)]
    for step in range(bits):
        sent = []
        for e in range(experts):
            bit = orders[e][step]
            axis = left[e].index(bit)
            shape = (2,) * len(left[e]) + (share, width)
            here = (index >> bit) % 2

            def half(side):
                total = None
                for term in held[e]:
                    piece = lax.dynamic_index_in_dim(
                        term.reshape(shape), side, axis=axis, keepdims=False
                    ).astype(jnp.float32)
                    total = piece if total is None else total + piece
                return total

            sent.append(half(1 - here).astype(jnp.bfloat16))
            held[e] = [half(here)]
            left[e].remove(bit)
        for e in range(experts):
            held[e].append(swap(sent[e], orders[e][step]))
        if step == min(1, bits - 1):
            held[-1], gate_rows = lax.optimization_barrier((held[-1], gate_rows))
    shares = [
        sum(term.astype(jnp.float32).reshape(share, width) for term in held[e])
        for e in range(experts)
    ]
    factor = jnp.stack(shares)
    grad = jnp.einsum(
        "efv,dv->efd",
        factor,
        projection.astype(jnp.float32),
        precision=lax.Precision.HIGHEST,
    )
    return grad, gate_rows


def local(
    hidden_states,
    expert_ids,
    router_weight,
    up_weight,
    down_weight,
    projection,
    teacher_scores,
    query_lengths,
    passage_lengths,
):
    tok_rows, width = hidden_states.shape
    here = up_weight.shape[0]
    first = lax.axis_index("exp") * here
    rows = spread_out(hidden_states)
    ids = spread_out(expert_ids.T)
    blocks = rows.shape[0]
    names = jnp.arange(E, dtype=jnp.int32)[None, :, None]
    is_first = (ids[:, :1] == names).astype(jnp.float32)
    is_second = (ids[:, 1:] == names).astype(jnp.float32)
    logits = jnp.einsum("de,ntd->net", router_weight, rows, preferred_element_type=jnp.float32)
    side = is_first - is_second
    first_gate = jax.nn.sigmoid(jnp.sum(logits * side, axis=1, keepdims=True))
    second_gate = 1.0 - first_gate
    named = is_first + is_second
    before = jnp.arange(tok_rows)[:, None] < jnp.arange(tok_rows)[None, :]
    slots = jnp.einsum(
        "net,tu->neu",
        named.astype(jnp.bfloat16),
        before.astype(jnp.bfloat16),
        preferred_element_type=jnp.float32,
    ).astype(jnp.int32)
    slots = jnp.where(named > 0, slots, -1)
    mine = lambda value: lax.dynamic_slice_in_dim(value, first, here, axis=1)
    slots_here = mine(slots)
    gates_here = mine(is_first * first_gate + is_second * second_gate)
    side_here = mine(side)
    hit = slots_here[:, :, None, :] == jnp.arange(CAP, dtype=jnp.int32)[None, None, :, None]
    pick = hit.astype(jnp.bfloat16)
    row_gate = jnp.sum(jnp.where(hit, gates_here[:, :, None, :], 0.0), axis=-1)
    row_gate = row_gate.transpose(1, 0, 2).reshape(here, blocks * CAP, 1)

    def to_slots(tokens):
        picked = jnp.einsum("nect,ntd->encd", pick, tokens, preferred_element_type=jnp.float32)
        return picked.astype(jnp.bfloat16).reshape(here, blocks * CAP, -1)

    def to_tokens(slot_rows):
        return jnp.einsum(
            "nect,encd->ntd",
            pick,
            slot_rows.reshape(here, blocks, CAP, width),
            preferred_element_type=jnp.float32,
        )

    expert_rows = to_slots(rows)
    preact = jnp.einsum(
        "erd,edf->erf", expert_rows, up_weight, preferred_element_type=jnp.float32
    )
    hidden = gelu_value(preact).astype(jnp.bfloat16)
    out = jnp.einsum("erf,efd->erd", hidden, down_weight, preferred_element_type=jnp.float32)
    mixed = bring_home(to_tokens((row_gate * out).astype(jnp.bfloat16)))
    mixed_rows = (hidden_states.astype(jnp.float32) + mixed).astype(jnp.bfloat16)
    projected = jnp.dot(mixed_rows, projection, preferred_element_type=jnp.float32)
    vec_norm = jnp.sqrt(jnp.sum(projected * projected, axis=-1, keepdims=True) + norm_eps)
    vectors = projected / vec_norm
    pairs_here = teacher_scores.shape[0]
    pair_kl, vector_grad = distill(
        vectors.reshape(pairs_here, -1, projected.shape[1]),
        teacher_scores,
        query_lengths,
        passage_lengths,
    )
    vector_grad = vector_grad.reshape(tok_rows, -1)
    radial = jnp.sum(vectors * vector_grad, axis=-1, keepdims=True)
    projected_grad = ((vector_grad - vectors * radial) / vec_norm).astype(jnp.bfloat16)
    mixed_grad = jnp.dot(projected_grad, projection.T, preferred_element_type=jnp.float32)
    pg_rows = to_slots(spread_out(projected_grad))
    grad_rows = jnp.einsum(
        "erv,dv->erd", pg_rows, projection, preferred_element_type=jnp.float32
    )
    out_grad = (row_gate * grad_rows).astype(jnp.bfloat16)
    gated = (row_gate * pg_rows.astype(jnp.float32)).astype(jnp.bfloat16)
    down_grad, out_grad = weight_grad(hidden, gated, projection, out_grad)
    gate_grad = jnp.sum(grad_rows * out, axis=-1).reshape(here, blocks, CAP).transpose(1, 0, 2)
    hit_grad = jnp.sum(jnp.where(hit, gate_grad[..., None], 0.0), axis=2)
    spread = jnp.sum(hit_grad * side_here, axis=1, keepdims=True) * first_gate * second_gate
    router_part = jnp.einsum(
        "net,de->ntd",
        spread * side,
        router_weight.astype(jnp.float32),
        precision=lax.Precision.HIGHEST,
    )
    hidden_grad = jnp.einsum(
        "erd,efd->erf", out_grad, down_weight, preferred_element_type=jnp.float32
    )
    pre_grad = (hidden_grad * gelu_slope(preact)).astype(jnp.bfloat16)
    row_grad = jnp.einsum(
        "erf,edf->erd", pre_grad, up_weight, preferred_element_type=jnp.float32
    ).astype(jnp.bfloat16)
    input_grad = (mixed_grad + bring_home(to_tokens(row_grad) + router_part)).astype(jnp.bfloat16)
    return (input_grad, down_grad, pair_kl)


def tall(value, rows):
    return jnp.concatenate(
        [value, jnp.zeros((rows - value.shape[0], value.shape[1]), value.dtype)], axis=0
    )


def dot_nn(left, right, precision=None):
    return lax.dot_general(
        left,
        right,
        (((1,), (0,)), ((), ())),
        precision=precision,
        preferred_element_type=jnp.float32,
    )


def dot_nt(left, right, precision=None):
    return lax.dot_general(
        left,
        right,
        (((1,), (1,)), ((), ())),
        precision=precision,
        preferred_element_type=jnp.float32,
    )


def layer_kernel(
    x_ref,
    ids_ref,
    rw_ref,
    up_hbm,
    down_hbm,
    proj_ref,
    teacher_ref,
    qlen_ref,
    plen_ref,
    grad_ref,
    down_grad_ref,
    kl_ref,
    up_v,
    down_v,
    rwp,
    tpad,
    px,
    pids,
    pick,
    spread_pick,
    row_gate,
    rows_ref,
    hid,
    slope,
    out_ref,
    gated_out,
    home,
    ret_send,
    ret_recv,
    pg,
    mixed_grad,
    pg_rows,
    back,
    coef,
    hitg,
    logit_hits,
    ret2_send,
    ret2_recv,
    core_send,
    core_recv,
    x_send,
    x_recv,
    z_send,
    z_recv,
    weight_sem,
    fetch_s,
    fetch_r,
    home_s,
    home_r,
    core_s,
    core_r,
    x_s,
    x_r,
    z_s,
    z_r,
):
    tokens, width = x_ref.shape
    here, _, units = up_v.shape
    vec = proj_ref.shape[1]
    lanes = vec
    queries = teacher_ref.shape[0]
    size = lax.axis_size("exp")
    reps = lax.axis_size("rep")
    depth = reps // 4
    rep = lax.axis_index("rep")
    own = lax.axis_index("exp")
    core, line, layer = rep % 2, (rep // 2) % 2, rep // 4
    share = units // reps
    wide = 2 * lanes
    tiles = units // wide

    peer = {"exp": 1 - own}
    core_peer = {"rep": rep + 1 - 2 * core}
    line_peer = {"rep": rep + 2 - 4 * line}

    def layer_peer(step):
        return {"rep": ((layer + step) % depth) * 4 + rep % 4}

    def remote(src, dst, send, recv, device):
        return pltpu.make_async_remote_copy(
            src_ref=src,
            dst_ref=dst,
            send_sem=send,
            recv_sem=recv,
            device_id=device,
            device_id_type=pl.DeviceIdType.MESH,
        )

    def up_copy(e):
        return pltpu.make_async_copy(up_hbm.at[e], up_v.at[e], weight_sem.at[0, e])

    def down_copy(e):
        return pltpu.make_async_copy(down_hbm.at[e], down_v.at[e], weight_sem.at[1, e])

    barrier = pltpu.get_barrier_semaphore()
    for device in [peer, core_peer, line_peer] + [layer_peer(k) for k in range(1, depth)]:
        pl.semaphore_signal(
            barrier, inc=1, device_id=device, device_id_type=pl.DeviceIdType.MESH
        )
    for e in range(here):
        up_copy(e).start()
    for e in range(here):
        down_copy(e).start()
    pl.semaphore_wait(barrier, 2 + depth)

    fetch_x = remote(x_ref, px, fetch_s.at[0], fetch_r.at[0], peer)
    fetch_ids = remote(ids_ref, pids, fetch_s.at[1], fetch_r.at[1], peer)
    fetch_ids.start()
    fetch_x.start()

    rwp[...] = jnp.zeros_like(rwp)
    rwp[:, 0:E] = rw_ref[...]
    earlier = lax.broadcasted_iota(jnp.int32, (tokens, tokens), 0)
    later = lax.broadcasted_iota(jnp.int32, (tokens, tokens), 1)
    before = jnp.where(earlier < later, 1.0, 0.0).astype(jnp.bfloat16)

    def mine(value):
        picked = value
        for side in range(1, size):
            moved = pltpu.roll(value, (E - side * here) % E, 0)
            picked = jnp.where(own == side, moved, picked)
        return picked

    def prepare(n, ids, tokens_rows):
        names = lax.broadcasted_iota(jnp.int32, (E, tokens), 0)
        is_first = jnp.where(ids[0:1] == names, 1.0, 0.0)
        is_second = jnp.where(ids[1:2] == names, 1.0, 0.0)
        logits = jnp.transpose(dot_nn(tokens_rows, rwp[...]))[0:E]
        side = is_first - is_second
        first_gate = jax.nn.sigmoid(jnp.sum(logits * side, axis=0, keepdims=True))
        second_gate = 1.0 - first_gate
        named = is_first + is_second
        slots = dot_nn(named.astype(jnp.bfloat16), before)
        slots = mine(jnp.where(named > 0, slots, -1.0))
        gates = mine(is_first * first_gate + is_second * second_gate)
        coef[n] = side * (first_gate * second_gate)
        hitg[n] = mine(side)
        place = lax.broadcasted_iota(jnp.int32, (CAP, tokens), 0).astype(jnp.float32)
        for e in range(here):
            hit = slots[e : e + 1] == place
            pick[n, e * CAP : (e + 1) * CAP, :] = jnp.where(hit, 1.0, 0.0).astype(jnp.bfloat16)
            row_gate[e, n * CAP : (n + 1) * CAP, :] = jnp.sum(
                jnp.where(hit, gates[e : e + 1], 0.0), axis=1, keepdims=True
            )
        by_token = jnp.transpose(tall(slots, lanes))
        column = lax.broadcasted_iota(jnp.int32, (tokens, here * CAP), 1)
        want = column
        have = jnp.broadcast_to(by_token[:, 0:1], column.shape)
        for e in range(1, here):
            inside = column >= e * CAP
            have = jnp.where(inside, by_token[:, e : e + 1], have)
            want = jnp.where(inside, column - e * CAP, want)
        spread_pick[n] = jnp.where(have == want.astype(jnp.float32), 1.0, 0.0).astype(
            jnp.bfloat16
        )
        gathered = dot_nn(pick[n], tokens_rows).astype(jnp.bfloat16)
        for e in range(here):
            rows_ref[e, n * CAP : (n + 1) * CAP, :] = gathered[e * CAP : (e + 1) * CAP]

    def rise(n, e):
        block = rows_ref[e, n * CAP : (n + 1) * CAP, :]
        for j in range(tiles):
            cut = slice(j * wide, (j + 1) * wide)
            preact = dot_nn(block, up_v[e, :, cut])
            half = 0.5 * (1.0 + lax.erf(preact * sqrt_half))
            hid[e, n * CAP : (n + 1) * CAP, cut] = (preact * half).astype(jnp.bfloat16)
            slope[e, n * CAP : (n + 1) * CAP, cut] = (
                half + preact * jnp.exp(-0.5 * preact * preact) * density_scale
            )

    prepare(0, ids_ref[...], x_ref[...])

    def first_pass(e, carry):
        up_copy(e).wait()
        rise(0, e)
        return carry

    lax.fori_loop(0, here, first_pass, 0)
    fetch_ids.wait_recv()
    fetch_x.wait_recv()
    prepare(1, pids[...], px[...])

    def second_pass(e, carry):
        rise(1, e)
        down_copy(e).wait()
        out = dot_nn(hid[e], down_v[e])
        out_ref[e] = out
        gated = (row_gate[e] * out).astype(jnp.bfloat16)
        gated_out[0, e] = gated[0:CAP]
        gated_out[1, e] = gated[CAP:]
        return carry

    lax.fori_loop(0, here, second_pass, 0)
    ret_send[...] = dot_nn(
        spread_pick[1], gated_out[1].reshape(here * CAP, width)
    ).astype(jnp.bfloat16)
    home_copy = remote(ret_send, ret_recv, home_s.at[0], home_r.at[0], peer)
    home_copy.start()
    home[...] = x_ref[...].astype(jnp.float32) + dot_nn(
        spread_pick[0], gated_out[0].reshape(here * CAP, width)
    )
    keys = lax.broadcasted_iota(jnp.int32, (queries, tokens), 1) - queries
    valid = jnp.where((keys >= 0) & (keys < plen_ref[0]), 1.0, 0.0)
    asked = jnp.where(
        lax.broadcasted_iota(jnp.int32, (queries, 1), 0) < qlen_ref[0], 1.0, 0.0
    )
    tpad[...] = jnp.zeros_like(tpad)
    tpad[:, 0 : tokens - queries] = teacher_ref[...]
    teacher_scores = pltpu.roll(tpad[...], queries, 1)
    teacher_exp = jnp.exp(teacher_scores) * valid
    teacher_total = jnp.sum(teacher_exp, axis=1, keepdims=True)
    teacher = teacher_exp / teacher_total
    log_teacher = teacher_scores - jnp.log(teacher_total)
    home_copy.wait_recv()
    mixed_rows = (home[...] + ret_recv[...].astype(jnp.float32)).astype(jnp.bfloat16)
    projected = dot_nn(mixed_rows, proj_ref[...])
    vec_norm = jnp.sqrt(jnp.sum(projected * projected, axis=1, keepdims=True) + norm_eps)
    vectors = projected / vec_norm
    best = lax.Precision.HIGHEST
    scores = score_scale * dot_nt(vectors[0:queries], vectors, best)
    student_exp = jnp.exp(scores) * valid
    student_total = jnp.sum(student_exp, axis=1, keepdims=True)
    student = student_exp / student_total
    log_student = scores - jnp.log(student_total)
    per_query = jnp.sum(teacher * (log_teacher - log_student), axis=1, keepdims=True)
    kl_ref[...] = jnp.sum(per_query * asked, axis=0, keepdims=True)
    score_grad = (student - teacher) * asked
    query_grad = dot_nn(score_grad, vectors, best)
    passage_grad = dot_nn(jnp.transpose(tall(score_grad, lanes)), vectors[0:lanes], best)
    vector_grad = score_scale * (passage_grad + tall(query_grad, tokens))
    radial = jnp.sum(vectors * vector_grad, axis=1, keepdims=True)
    pg[0] = ((vector_grad - vectors * radial) / vec_norm).astype(jnp.bfloat16)
    pg_copy = remote(pg.at[0], pg.at[1], home_s.at[1], home_r.at[1], peer)
    pg_copy.start()

    def take_rows(n):
        picked = dot_nn(pick[n], pg[n]).astype(jnp.bfloat16)
        for e in range(here):
            pg_rows[e, n * CAP : (n + 1) * CAP, :] = picked[e * CAP : (e + 1) * CAP]

    take_rows(0)
    mixed_grad[...] = dot_nt(pg[0], proj_ref[...])
    pg_copy.wait_recv()
    take_rows(1)

    def core_copy(e):
        return remote(
            core_send.at[1 - core, e], core_recv.at[e], core_s.at[e], core_r.at[e], core_peer
        )

    def line_copy(e):
        return remote(x_send.at[1 - line, e], x_recv.at[e], x_s.at[e], x_r.at[e], line_peer)

    def layer_copy(step, e):
        return remote(
            z_send.at[(layer + step) % depth, e],
            z_recv.at[step - 1, e],
            z_s.at[step - 1, e],
            z_r.at[step - 1, e],
            layer_peer(step),
        )

    def factor(e, carry):
        gated = row_gate[e] * pg_rows[e].astype(jnp.float32)
        turned = jnp.transpose(gated).astype(jnp.bfloat16)
        product = dot_nn(turned, hid[e]).astype(jnp.bfloat16)
        for r in range(reps):
            core_send[r % 2, e, r // 2] = product[:, r * share : (r + 1) * share]
        core_copy(e).start()
        return carry

    lax.fori_loop(0, here, factor, 0)

    def after_core(e):
        core_copy(e).wait_recv()
        for k in range(2 * depth):
            total = core_send[core, e, k].astype(jnp.float32) + core_recv[e, k].astype(
                jnp.float32
            )
            x_send[k % 2, e, k // 2] = total.astype(jnp.bfloat16)
        line_copy(e).start()

    def line_sum(e, k):
        return x_send[line, e, k].astype(jnp.float32) + x_recv[e, k].astype(jnp.float32)

    def after_line(e):
        line_copy(e).wait_recv()
        for k in range(depth):
            z_send[k, e] = line_sum(e, k).astype(jnp.bfloat16)
        for step in range(1, depth):
            layer_copy(step, e).start()

    def fall(e, carry):
        upstream = dot_nt(pg_rows[e], proj_ref[...])
        grad = jnp.sum(upstream * out_ref[e], axis=1, keepdims=True)
        place = lax.broadcasted_iota(jnp.int32, (CAP, tokens), 0).astype(jnp.float32)
        for n in range(2):
            hits = jnp.sum(
                pick[n, pl.ds(pl.multiple_of(e * CAP, CAP), CAP), :].astype(jnp.float32)
                * grad[n * CAP : (n + 1) * CAP],
                axis=0,
                keepdims=True,
            )
            logit_hits[n] += hits * hitg[n, pl.ds(e, 1), :]
        out_grad = (row_gate[e] * upstream).astype(jnp.bfloat16)
        total = None
        for j in range(tiles):
            cut = slice(j * wide, (j + 1) * wide)
            hidden_grad = dot_nt(out_grad, down_v[e, cut, :])
            pre_grad = (hidden_grad * slope[e, :, cut]).astype(jnp.bfloat16)
            part = dot_nt(pre_grad, up_v[e, :, cut])
            total = part if total is None else total + part
        rounded = total.astype(jnp.bfloat16)
        back[0, e] = rounded[0:CAP]
        back[1, e] = rounded[CAP:]

        @pl.when(e == 0)
        def _():
            def each(k, inner):
                after_core(k)
                return inner

            lax.fori_loop(0, here, each, 0)

        @pl.when(e >= 2)
        def _():
            after_line(e - 2)

        return carry

    logit_hits[...] = jnp.zeros_like(logit_hits)
    lax.fori_loop(0, here, fall, 0)

    def into_tokens(n):
        logit_grad = jnp.transpose(tall(logit_hits[n] * coef[n], lanes))
        return dot_nn(spread_pick[n], back[n].reshape(here * CAP, width)) + dot_nt(
            logit_grad, rwp[...].astype(jnp.float32), best
        )

    ret2_send[...] = into_tokens(1).astype(jnp.bfloat16)
    last_copy = remote(ret2_send, ret2_recv, home_s.at[2], home_r.at[2], peer)
    last_copy.start()
    mixed_grad[...] += into_tokens(0)

    def finish(e, carry):
        total = line_sum(e, layer)
        for step in range(1, depth):
            layer_copy(step, e).wait_recv()
            total = total + z_recv[step - 1, e].astype(jnp.float32)
        turned = jnp.transpose(total)
        high = turned.astype(jnp.bfloat16)
        low = (turned - high.astype(jnp.float32)).astype(jnp.bfloat16)
        down_grad_ref[e] = dot_nt(high, proj_ref[...]) + dot_nt(low, proj_ref[...])
        return carry

    def trailing(e, carry):
        after_line(e)
        return carry

    lax.fori_loop(max(here - 2, 0), here, trailing, 0)
    last_copy.wait_recv()
    grad_ref[...] = (mixed_grad[...] + ret2_recv[...].astype(jnp.float32)).astype(jnp.bfloat16)
    lax.fori_loop(0, here, finish, 0)

    fetch_ids.wait_send()
    fetch_x.wait_send()
    home_copy.wait_send()
    pg_copy.wait_send()
    last_copy.wait_send()

    def drain(e, carry):
        core_copy(e).wait_send()
        line_copy(e).wait_send()
        for step in range(1, depth):
            layer_copy(step, e).wait_send()
        return carry

    lax.fori_loop(0, here, drain, 0)


def fused(
    hidden_states,
    expert_ids,
    router_weight,
    up_weight,
    down_weight,
    projection,
    teacher_scores,
    query_lengths,
    passage_lengths,
):
    tokens, width = hidden_states.shape
    here, _, units = up_weight.shape
    vec = projection.shape[1]
    queries = teacher_scores.shape[1]
    depth = lax.axis_size("rep") // 4
    rows = 2 * CAP
    share = units // lax.axis_size("rep")
    vmem = pl.BlockSpec(memory_space=pltpu.VMEM)
    smem = pl.BlockSpec(memory_space=pltpu.SMEM)
    hbm = pl.BlockSpec(memory_space=pl.ANY)
    half, full = jnp.bfloat16, jnp.float32
    dma = pltpu.SemaphoreType.DMA
    scratch = [
        pltpu.VMEM((here, width, units), half),
        pltpu.VMEM((here, units, width), half),
        pltpu.VMEM((width, vec), half),
        pltpu.VMEM((queries, tokens), full),
        pltpu.VMEM((tokens, width), half),
        pltpu.VMEM((2, tokens), jnp.int32),
        pltpu.VMEM((2, here * CAP, tokens), half),
        pltpu.VMEM((2, tokens, here * CAP), half),
        pltpu.VMEM((here, rows, 1), full),
        pltpu.VMEM((here, rows, width), half),
        pltpu.VMEM((here, rows, units), half),
        pltpu.VMEM((here, rows, units), full),
        pltpu.VMEM((here, rows, width), full),
        pltpu.VMEM((2, here, CAP, width), half),
        pltpu.VMEM((tokens, width), full),
        pltpu.VMEM((tokens, width), half),
        pltpu.VMEM((tokens, width), half),
        pltpu.VMEM((2, tokens, vec), half),
        pltpu.VMEM((tokens, width), full),
        pltpu.VMEM((here, rows, vec), half),
        pltpu.VMEM((2, here, CAP, width), half),
        pltpu.VMEM((2, E, tokens), full),
        pltpu.VMEM((2, E, tokens), full),
        pltpu.VMEM((2, 1, tokens), full),
        pltpu.VMEM((tokens, width), half),
        pltpu.VMEM((tokens, width), half),
        pltpu.VMEM((2, here, 2 * depth, vec, share), half),
        pltpu.VMEM((here, 2 * depth, vec, share), half),
        pltpu.VMEM((2, here, depth, vec, share), half),
        pltpu.VMEM((here, depth, vec, share), half),
        pltpu.VMEM((depth, here, vec, share), half),
        pltpu.VMEM((depth - 1, here, vec, share), half),
        dma((2, here)),
        dma((2,)),
        dma((2,)),
        dma((3,)),
        dma((3,)),
        dma((here,)),
        dma((here,)),
        dma((here,)),
        dma((here,)),
        dma((depth - 1, here)),
        dma((depth - 1, here)),
    ]
    input_grad, down_grad, pair_kl = pl.pallas_call(
        layer_kernel,
        out_shape=(
            jax.ShapeDtypeStruct((tokens, width), half),
            jax.ShapeDtypeStruct((here, share, width), full),
            jax.ShapeDtypeStruct((1, 1), full),
        ),
        in_specs=[vmem, vmem, vmem, hbm, hbm, vmem, vmem, smem, smem],
        out_specs=(vmem, vmem, vmem),
        scratch_shapes=scratch,
        compiler_params=pltpu.CompilerParams(
            collective_id=0, has_side_effects=True, vmem_limit_bytes=56 * 1024 * 1024
        ),
    )(
        hidden_states,
        expert_ids.T,
        router_weight,
        up_weight,
        down_weight,
        projection,
        teacher_scores[0],
        query_lengths,
        passage_lengths,
    )
    return input_grad, down_grad, pair_kl.reshape(1)


def fits(mesh, hidden_states, up_weight, projection, teacher_scores):
    reps, size = mesh.shape["rep"], mesh.shape["exp"]
    pairs, queries, _ = teacher_scores.shape
    tokens = hidden_states.shape[0] // (reps * size)
    experts, width, units = up_weight.shape
    vec = projection.shape[1]
    return (
        size == 2
        and reps % 4 == 0
        and reps >= 8
        and experts == E
        and pairs == reps * size
        and units == reps * vec
        and vec == 128
        and width % 128 == 0
        and tokens % 128 == 0
        and queries <= 128
        and experts // size >= 2
    )


def solution(mesh):
    placed = (
        P(("rep", "exp"), None),
        P(("rep", "exp"), None),
        P(),
        P("exp", None, None),
        P("exp", None, None),
        P(),
        P(("rep", "exp"), None, None),
        P(("rep", "exp")),
        P(("rep", "exp")),
    )

    def program(*arrays):
        body = fused if fits(mesh, arrays[0], arrays[3], arrays[5], arrays[6]) else local
        return jax.shard_map(
            body,
            mesh=mesh,
            in_specs=placed,
            out_specs=(P(("rep", "exp"), None), P("exp", "rep", None), P(("rep", "exp"))),
            check_vma=False,
        )(*arrays)

    return program
```

```python
import jax
import jax.numpy as jnp
from jax import lax
from jax.experimental import pallas as pl
from jax.experimental.pallas import tpu as pltpu
from jax.sharding import PartitionSpec as P

E = 8
LQ = 32
LP = 224
CAP = 96


score_scale = 20.0
norm_eps = 1e-06
sqrt_half = 0.7071067811865476
density_scale = 0.3989422804014327


def gelu_value(preact):
    return 0.5 * preact * (1.0 + lax.erf(preact * sqrt_half))


def gelu_slope(preact):
    return (
        0.5 * (1.0 + lax.erf(preact * sqrt_half))
        + preact * jnp.exp(-0.5 * preact * preact) * density_scale
    )


def distill(vectors, teacher_scores, query_lengths, passage_lengths):
    queries = vectors[:, :LQ]
    passages = vectors[:, LQ:]
    scores = score_scale * jnp.einsum(
        "pqv,pkv->pqk", queries, passages, precision=lax.Precision.HIGHEST
    )
    query_mask = (jnp.arange(LQ, dtype=jnp.int32)[None, :] < query_lengths[:, None]).astype(
        jnp.float32
    )
    passage_mask = (jnp.arange(LP, dtype=jnp.int32)[None, :] < passage_lengths[:, None]).astype(
        jnp.float32
    )
    student_exp = jnp.exp(scores) * passage_mask[:, None, :]
    student_total = jnp.sum(student_exp, axis=-1, keepdims=True)
    student = student_exp / student_total
    log_student = scores - jnp.log(student_total)
    teacher_exp = jnp.exp(teacher_scores) * passage_mask[:, None, :]
    teacher_total = jnp.sum(teacher_exp, axis=-1, keepdims=True)
    teacher = teacher_exp / teacher_total
    log_teacher = teacher_scores - jnp.log(teacher_total)
    per_query = jnp.sum(teacher * (log_teacher - log_student), axis=-1)
    pair_kl = jnp.sum(per_query * query_mask, axis=-1)
    score_grad = (student - teacher) * query_mask[:, :, None]
    query_grad = score_scale * jnp.einsum(
        "pqk,pkv->pqv", score_grad, passages, precision=lax.Precision.HIGHEST
    )
    passage_grad = score_scale * jnp.einsum(
        "pqk,pqv->pkv", score_grad, queries, precision=lax.Precision.HIGHEST
    )
    return (pair_kl, jnp.concatenate([query_grad, passage_grad], axis=1))


def fetch(block, shift):
    size = lax.axis_size("exp")
    return lax.ppermute(block, "exp", [(i, (i - shift) % size) for i in range(size)])


def give_back(block, shift):
    size = lax.axis_size("exp")
    return lax.ppermute(block, "exp", [(i, (i + shift) % size) for i in range(size)])


def spread_out(block):
    size = lax.axis_size("exp")
    return jnp.stack([block] + [fetch(block, shift) for shift in range(1, size)])


def bring_home(parts):
    total = parts[0]
    for shift in range(1, parts.shape[0]):
        total = total + give_back(parts[shift].astype(jnp.bfloat16), shift).astype(jnp.float32)
    return total


def halving_orders(bits, experts):
    near = list(range(bits))
    late = [0] + list(range(2, bits)) + [1] if bits > 2 else near
    return [late if expert % 4 == 3 else near for expert in range(experts)]


def weight_grad(hidden, gated, projection, gate_rows):
    size = lax.axis_size("rep")
    bits = size.bit_length() - 1
    experts, _, units = hidden.shape
    width = gated.shape[-1]
    share = units // size
    index = lax.axis_index("rep")
    product = jnp.einsum(
        "erf,erv->efv", hidden, gated, preferred_element_type=jnp.float32
    ).astype(jnp.bfloat16)

    def swap(block, bit):
        return lax.ppermute(block, "rep", [(i, i ^ (1 << bit)) for i in range(size)])

    orders = halving_orders(bits, experts)
    left = [list(range(bits - 1, -1, -1)) for _ in range(experts)]
    held = [[product[e]] for e in range(experts)]
    for step in range(bits):
        sent = []
        for e in range(experts):
            bit = orders[e][step]
            axis = left[e].index(bit)
            shape = (2,) * len(left[e]) + (share, width)
            here = (index >> bit) % 2

            def half(side):
                total = None
                for term in held[e]:
                    piece = lax.dynamic_index_in_dim(
                        term.reshape(shape), side, axis=axis, keepdims=False
                    ).astype(jnp.float32)
                    total = piece if total is None else total + piece
                return total

            sent.append(half(1 - here).astype(jnp.bfloat16))
            held[e] = [half(here)]
            left[e].remove(bit)
        for e in range(experts):
            held[e].append(swap(sent[e], orders[e][step]))
        if step == min(1, bits - 1):
            held[-1], gate_rows = lax.optimization_barrier((held[-1], gate_rows))
    shares = [
        sum(term.astype(jnp.float32).reshape(share, width) for term in held[e])
        for e in range(experts)
    ]
    factor = jnp.stack(shares)
    grad = jnp.einsum(
        "efv,dv->efd",
        factor,
        projection.astype(jnp.float32),
        precision=lax.Precision.HIGHEST,
    )
    return grad, gate_rows


def local(
    hidden_states,
    expert_ids,
    router_weight,
    up_weight,
    down_weight,
    projection,
    teacher_scores,
    query_lengths,
    passage_lengths,
):
    tok_rows, width = hidden_states.shape
    here = up_weight.shape[0]
    first = lax.axis_index("exp") * here
    rows = spread_out(hidden_states)
    ids = spread_out(expert_ids.T)
    blocks = rows.shape[0]
    names = jnp.arange(E, dtype=jnp.int32)[None, :, None]
    is_first = (ids[:, :1] == names).astype(jnp.float32)
    is_second = (ids[:, 1:] == names).astype(jnp.float32)
    logits = jnp.einsum("de,ntd->net", router_weight, rows, preferred_element_type=jnp.float32)
    side = is_first - is_second
    first_gate = jax.nn.sigmoid(jnp.sum(logits * side, axis=1, keepdims=True))
    second_gate = 1.0 - first_gate
    named = is_first + is_second
    before = jnp.arange(tok_rows)[:, None] < jnp.arange(tok_rows)[None, :]
    slots = jnp.einsum(
        "net,tu->neu",
        named.astype(jnp.bfloat16),
        before.astype(jnp.bfloat16),
        preferred_element_type=jnp.float32,
    ).astype(jnp.int32)
    slots = jnp.where(named > 0, slots, -1)
    mine = lambda value: lax.dynamic_slice_in_dim(value, first, here, axis=1)
    slots_here = mine(slots)
    gates_here = mine(is_first * first_gate + is_second * second_gate)
    side_here = mine(side)
    hit = slots_here[:, :, None, :] == jnp.arange(CAP, dtype=jnp.int32)[None, None, :, None]
    pick = hit.astype(jnp.bfloat16)
    row_gate = jnp.sum(jnp.where(hit, gates_here[:, :, None, :], 0.0), axis=-1)
    row_gate = row_gate.transpose(1, 0, 2).reshape(here, blocks * CAP, 1)

    def to_slots(tokens):
        picked = jnp.einsum("nect,ntd->encd", pick, tokens, preferred_element_type=jnp.float32)
        return picked.astype(jnp.bfloat16).reshape(here, blocks * CAP, -1)

    def to_tokens(slot_rows):
        return jnp.einsum(
            "nect,encd->ntd",
            pick,
            slot_rows.reshape(here, blocks, CAP, width),
            preferred_element_type=jnp.float32,
        )

    expert_rows = to_slots(rows)
    preact = jnp.einsum(
        "erd,edf->erf", expert_rows, up_weight, preferred_element_type=jnp.float32
    )
    hidden = gelu_value(preact).astype(jnp.bfloat16)
    out = jnp.einsum("erf,efd->erd", hidden, down_weight, preferred_element_type=jnp.float32)
    mixed = bring_home(to_tokens((row_gate * out).astype(jnp.bfloat16)))
    mixed_rows = (hidden_states.astype(jnp.float32) + mixed).astype(jnp.bfloat16)
    projected = jnp.dot(mixed_rows, projection, preferred_element_type=jnp.float32)
    vec_norm = jnp.sqrt(jnp.sum(projected * projected, axis=-1, keepdims=True) + norm_eps)
    vectors = projected / vec_norm
    pairs_here = teacher_scores.shape[0]
    pair_kl, vector_grad = distill(
        vectors.reshape(pairs_here, -1, projected.shape[1]),
        teacher_scores,
        query_lengths,
        passage_lengths,
    )
    vector_grad = vector_grad.reshape(tok_rows, -1)
    radial = jnp.sum(vectors * vector_grad, axis=-1, keepdims=True)
    projected_grad = ((vector_grad - vectors * radial) / vec_norm).astype(jnp.bfloat16)
    mixed_grad = jnp.dot(projected_grad, projection.T, preferred_element_type=jnp.float32)
    pg_rows = to_slots(spread_out(projected_grad))
    grad_rows = jnp.einsum(
        "erv,dv->erd", pg_rows, projection, preferred_element_type=jnp.float32
    )
    out_grad = (row_gate * grad_rows).astype(jnp.bfloat16)
    gated = (row_gate * pg_rows.astype(jnp.float32)).astype(jnp.bfloat16)
    down_grad, out_grad = weight_grad(hidden, gated, projection, out_grad)
    gate_grad = jnp.sum(grad_rows * out, axis=-1).reshape(here, blocks, CAP).transpose(1, 0, 2)
    hit_grad = jnp.sum(jnp.where(hit, gate_grad[..., None], 0.0), axis=2)
    spread = jnp.sum(hit_grad * side_here, axis=1, keepdims=True) * first_gate * second_gate
    router_part = jnp.einsum(
        "net,de->ntd",
        spread * side,
        router_weight.astype(jnp.float32),
        precision=lax.Precision.HIGHEST,
    )
    hidden_grad = jnp.einsum(
        "erd,efd->erf", out_grad, down_weight, preferred_element_type=jnp.float32
    )
    pre_grad = (hidden_grad * gelu_slope(preact)).astype(jnp.bfloat16)
    row_grad = jnp.einsum(
        "erf,edf->erd", pre_grad, up_weight, preferred_element_type=jnp.float32
    ).astype(jnp.bfloat16)
    input_grad = (mixed_grad + bring_home(to_tokens(row_grad) + router_part)).astype(jnp.bfloat16)
    return (input_grad, down_grad, pair_kl)


def tall(value, rows):
    return jnp.concatenate(
        [value, jnp.zeros((rows - value.shape[0], value.shape[1]), value.dtype)], axis=0
    )


def dot_nn(left, right, precision=None):
    return lax.dot_general(
        left,
        right,
        (((1,), (0,)), ((), ())),
        precision=precision,
        preferred_element_type=jnp.float32,
    )


def dot_nt(left, right, precision=None):
    return lax.dot_general(
        left,
        right,
        (((1,), (1,)), ((), ())),
        precision=precision,
        preferred_element_type=jnp.float32,
    )


def layer_kernel(
    x_ref,
    ids_ref,
    rw_ref,
    up_hbm,
    down_hbm,
    proj_ref,
    teacher_ref,
    qlen_ref,
    plen_ref,
    grad_ref,
    factor_ref,
    kl_ref,
    up_v,
    down_v,
    rwp,
    tpad,
    px,
    pids,
    pick,
    spread_pick,
    row_gate,
    rows_ref,
    hid,
    slope,
    held,
    out_ref,
    gated_out,
    home,
    ret_send,
    ret_recv,
    pg,
    mixed_grad,
    pg_rows,
    back,
    coef,
    hitg,
    logit_hits,
    ret2_send,
    ret2_recv,
    core_send,
    core_recv,
    x_send,
    x_recv,
    z_send,
    z_recv,
    weight_sem,
    fetch_s,
    fetch_r,
    home_s,
    home_r,
    core_s,
    core_r,
    x_s,
    x_r,
    z_s,
    z_r,
):
    tokens, width = x_ref.shape
    here, _, units = up_v.shape
    vec = proj_ref.shape[1]
    lanes = vec
    queries = teacher_ref.shape[0]
    size = lax.axis_size("exp")
    reps = lax.axis_size("rep")
    depth = reps // 4
    rep = lax.axis_index("rep")
    own = lax.axis_index("exp")
    core, line, layer = rep % 2, (rep // 2) % 2, rep // 4
    share = units // reps
    wide = 2 * lanes
    tiles = units // wide

    peer = {"exp": 1 - own}
    core_peer = {"rep": rep + 1 - 2 * core}
    line_peer = {"rep": rep + 2 - 4 * line}

    def layer_peer(step):
        return {"rep": ((layer + step) % depth) * 4 + rep % 4}

    def remote(src, dst, send, recv, device):
        return pltpu.make_async_remote_copy(
            src_ref=src,
            dst_ref=dst,
            send_sem=send,
            recv_sem=recv,
            device_id=device,
            device_id_type=pl.DeviceIdType.MESH,
        )

    def up_copy(e):
        return pltpu.make_async_copy(up_hbm.at[e], up_v.at[e], weight_sem.at[0, e])

    def down_copy(e):
        return pltpu.make_async_copy(down_hbm.at[e], down_v.at[e], weight_sem.at[1, e])

    barrier = pltpu.get_barrier_semaphore()
    for device in [peer, core_peer, line_peer] + [layer_peer(k) for k in range(1, depth)]:
        pl.semaphore_signal(
            barrier, inc=1, device_id=device, device_id_type=pl.DeviceIdType.MESH
        )
    for e in range(here):
        up_copy(e).start()
    for e in range(here):
        down_copy(e).start()
    pl.semaphore_wait(barrier, 2 + depth)

    fetch_x = remote(x_ref, px, fetch_s.at[0], fetch_r.at[0], peer)
    fetch_ids = remote(ids_ref, pids, fetch_s.at[1], fetch_r.at[1], peer)
    fetch_ids.start()
    fetch_x.start()

    rwp[...] = tall(rw_ref[...].astype(jnp.float32), lanes)
    earlier = lax.broadcasted_iota(jnp.int32, (tokens, tokens), 0)
    later = lax.broadcasted_iota(jnp.int32, (tokens, tokens), 1)
    before = jnp.where(earlier < later, 1.0, 0.0).astype(jnp.bfloat16)

    def mine(value):
        picked = value
        for side in range(1, size):
            moved = pltpu.roll(value, (E - side * here) % E, 0)
            picked = jnp.where(own == side, moved, picked)
        return picked

    def prepare(n, ids, tokens_rows):
        names = lax.broadcasted_iota(jnp.int32, (E, tokens), 0)
        is_first = jnp.where(ids[0:1] == names, 1.0, 0.0)
        is_second = jnp.where(ids[1:2] == names, 1.0, 0.0)
        logits = dot_nt(rw_ref[...], tokens_rows)
        side = is_first - is_second
        first_gate = jax.nn.sigmoid(jnp.sum(logits * side, axis=0, keepdims=True))
        second_gate = 1.0 - first_gate
        named = is_first + is_second
        slots = dot_nn(named.astype(jnp.bfloat16), before)
        slots = mine(jnp.where(named > 0, slots, -1.0))
        gates = mine(is_first * first_gate + is_second * second_gate)
        coef[n] = side * (first_gate * second_gate)
        hitg[n] = mine(side)
        place = lax.broadcasted_iota(jnp.int32, (CAP, tokens), 0).astype(jnp.float32)
        for e in range(here):
            hit = slots[e : e + 1] == place
            pick[n, e * CAP : (e + 1) * CAP, :] = jnp.where(hit, 1.0, 0.0).astype(jnp.bfloat16)
            row_gate[e, n * CAP : (n + 1) * CAP, :] = jnp.sum(
                jnp.where(hit, gates[e : e + 1], 0.0), axis=1, keepdims=True
            )
        by_token = jnp.transpose(tall(slots, lanes))
        column = lax.broadcasted_iota(jnp.int32, (tokens, here * CAP), 1)
        want = column
        have = jnp.broadcast_to(by_token[:, 0:1], column.shape)
        for e in range(1, here):
            inside = column >= e * CAP
            have = jnp.where(inside, by_token[:, e : e + 1], have)
            want = jnp.where(inside, column - e * CAP, want)
        spread_pick[n] = jnp.where(have == want.astype(jnp.float32), 1.0, 0.0).astype(
            jnp.bfloat16
        )
        gathered = dot_nn(pick[n], tokens_rows).astype(jnp.bfloat16)
        for e in range(here):
            rows_ref[e, n * CAP : (n + 1) * CAP, :] = gathered[e * CAP : (e + 1) * CAP]

    def density(preact):
        return preact * jnp.exp(-0.5 * preact * preact) * density_scale

    def rise(n, e):
        block = rows_ref[e, n * CAP : (n + 1) * CAP, :]
        for j in range(tiles):
            cut = slice(j * wide, (j + 1) * wide)
            preact = dot_nn(block, up_v[e, :, cut])
            half = 0.5 * (1.0 + lax.erf(preact * sqrt_half))
            hid[e, n * CAP : (n + 1) * CAP, cut] = (preact * half).astype(jnp.bfloat16)
            if n == 0:
                half = half + density(preact)
            else:
                held[e, :, cut] = preact
            slope[e, n * CAP : (n + 1) * CAP, cut] = half

    prepare(0, ids_ref[...], x_ref[...])

    def first_pass(e, carry):
        up_copy(e).wait()
        rise(0, e)
        return carry

    lax.fori_loop(0, here, first_pass, 0)
    fetch_ids.wait_recv()
    fetch_x.wait_recv()
    prepare(1, pids[...], px[...])

    def second_pass(e, carry):
        rise(1, e)
        down_copy(e).wait()
        out = dot_nn(hid[e], down_v[e])
        out_ref[e] = out
        gated = (row_gate[e] * out).astype(jnp.bfloat16)
        gated_out[0, e] = gated[0:CAP]
        gated_out[1, e] = gated[CAP:]
        return carry

    lax.fori_loop(0, here, second_pass, 0)
    def to_vectors(n):
        rows = dot_nn(gated_out[n].reshape(here * CAP, width), proj_ref[...])
        return dot_nn(spread_pick[n], rows.astype(jnp.bfloat16))

    ret_send[...] = to_vectors(1).astype(jnp.bfloat16)
    home_copy = remote(ret_send, ret_recv, home_s.at[0], home_r.at[0], peer)
    home_copy.start()
    home[...] = dot_nn(x_ref[...], proj_ref[...]) + to_vectors(0)

    def steepen(e, carry):
        for j in range(tiles):
            cut = slice(j * wide, (j + 1) * wide)
            slope[e, CAP:, cut] += density(held[e, :, cut])
        return carry

    lax.fori_loop(0, here, steepen, 0)
    keys = lax.broadcasted_iota(jnp.int32, (queries, tokens), 1) - queries
    valid = jnp.where((keys >= 0) & (keys < plen_ref[...]), 1.0, 0.0)
    asked = jnp.where(
        lax.broadcasted_iota(jnp.int32, (queries, 1), 0) < qlen_ref[...], 1.0, 0.0
    )
    tpad[...] = jnp.zeros_like(tpad)
    tpad[:, 0 : tokens - queries] = teacher_ref[...]
    teacher_scores = pltpu.roll(tpad[...], queries, 1)
    teacher_exp = jnp.exp(teacher_scores) * valid
    teacher_total = jnp.sum(teacher_exp, axis=1, keepdims=True)
    teacher = teacher_exp / teacher_total
    log_teacher = teacher_scores - jnp.log(teacher_total)
    home_copy.wait_recv()
    projected = home[...] + ret_recv[...].astype(jnp.float32)
    vec_norm = jnp.sqrt(jnp.sum(projected * projected, axis=1, keepdims=True) + norm_eps)
    vectors = projected / vec_norm
    best = lax.Precision.HIGHEST
    scores = score_scale * dot_nt(vectors[0:queries], vectors, best)
    student_exp = jnp.exp(scores) * valid
    student_total = jnp.sum(student_exp, axis=1, keepdims=True)
    student = student_exp / student_total
    log_student = scores - jnp.log(student_total)
    per_query = jnp.sum(teacher * (log_teacher - log_student), axis=1, keepdims=True)
    kl_ref[...] = jnp.sum(per_query * asked, axis=0, keepdims=True)
    score_grad = (student - teacher) * asked
    query_grad = dot_nn(score_grad, vectors, best)
    passage_grad = dot_nn(jnp.transpose(tall(score_grad, lanes)), vectors[0:lanes], best)
    vector_grad = score_scale * (passage_grad + tall(query_grad, tokens))
    radial = jnp.sum(vectors * vector_grad, axis=1, keepdims=True)
    pg[0] = ((vector_grad - vectors * radial) / vec_norm).astype(jnp.bfloat16)
    pg_copy = remote(pg.at[0], pg.at[1], home_s.at[1], home_r.at[1], peer)
    pg_copy.start()

    def take_rows(n):
        picked = dot_nn(pick[n], pg[n]).astype(jnp.bfloat16)
        for e in range(here):
            pg_rows[e, n * CAP : (n + 1) * CAP, :] = picked[e * CAP : (e + 1) * CAP]

    take_rows(0)
    mixed_grad[...] = dot_nt(pg[0], proj_ref[...])
    pg_copy.wait_recv()
    take_rows(1)

    parts = core_send.shape[1] // here
    chunks = here * parts
    slab = vec // parts

    def core_copy(e):
        return remote(
            core_send.at[1 - core, e], core_recv.at[e], core_s.at[e], core_r.at[e], core_peer
        )

    def line_copy(e):
        return remote(x_send.at[1 - line, e], x_recv.at[e], x_s.at[e], x_r.at[e], line_peer)

    def layer_copy(step, e):
        return remote(
            z_send.at[(layer + step) % depth, e],
            z_recv.at[step - 1, e],
            z_s.at[step - 1, e],
            z_r.at[step - 1, e],
            layer_peer(step),
        )

    def factor(e, carry):
        gated = row_gate[e] * pg_rows[e].astype(jnp.float32)
        turned = jnp.transpose(gated).astype(jnp.bfloat16)
        product = dot_nn(turned, hid[e]).astype(jnp.bfloat16)
        for p in range(parts):
            for r in range(reps):
                core_send[r % 2, e * parts + p, r // 2] = product[
                    p * slab : (p + 1) * slab, r * share : (r + 1) * share
                ]
            core_copy(e * parts + p).start()

        @pl.when(e >= 1)
        def _():
            for p in range(parts):
                after_core((e - 1) * parts + p)

        return carry

    def after_core(e):
        core_copy(e).wait_recv()
        for k in range(2 * depth):
            total = core_send[core, e, k].astype(jnp.float32) + core_recv[e, k].astype(
                jnp.float32
            )
            x_send[k % 2, e, k // 2] = total.astype(jnp.bfloat16)
        line_copy(e).start()

    lax.fori_loop(0, here, factor, 0)
    for p in range(parts):
        after_core((here - 1) * parts + p)

    def line_sum(e, k):
        return x_send[line, e, k].astype(jnp.float32) + x_recv[e, k].astype(jnp.float32)

    def after_line(e):
        line_copy(e).wait_recv()
        for k in range(depth):
            z_send[k, e] = line_sum(e, k).astype(jnp.bfloat16)
        for step in range(1, depth):
            layer_copy(step, e).start()

    def fall(e, carry):
        upstream = dot_nt(pg_rows[e], proj_ref[...])
        grad = jnp.sum(upstream * out_ref[e], axis=1, keepdims=True)
        place = lax.broadcasted_iota(jnp.int32, (CAP, tokens), 0).astype(jnp.float32)
        for n in range(2):
            hits = jnp.sum(
                pick[n, pl.ds(pl.multiple_of(e * CAP, CAP), CAP), :].astype(jnp.float32)
                * grad[n * CAP : (n + 1) * CAP],
                axis=0,
                keepdims=True,
            )
            logit_hits[n] += hits * hitg[n, pl.ds(e, 1), :]
        out_grad = (row_gate[e] * upstream).astype(jnp.bfloat16)
        total = None
        for j in range(tiles):
            cut = slice(j * wide, (j + 1) * wide)
            hidden_grad = dot_nt(out_grad, down_v[e, cut, :])
            pre_grad = (hidden_grad * slope[e, :, cut]).astype(jnp.bfloat16)
            part = dot_nt(pre_grad, up_v[e, :, cut])
            total = part if total is None else total + part
        rounded = total.astype(jnp.bfloat16)
        back[0, e] = rounded[0:CAP]
        back[1, e] = rounded[CAP:]

        lax.fori_loop(e * taken // here, (e + 1) * taken // here, line_step, 0)
        return carry

    taken = max(chunks - 3, 1)

    def line_step(k, carry):
        after_line(k)
        return carry

    logit_hits[...] = jnp.zeros_like(logit_hits)
    lax.fori_loop(0, here, fall, 0)

    def into_tokens(n):
        logit_grad = jnp.transpose(tall(logit_hits[n] * coef[n], lanes))
        return dot_nn(spread_pick[n], back[n].reshape(here * CAP, width)) + dot_nn(
            logit_grad, rwp[...], best
        )

    ret2_send[...] = into_tokens(1).astype(jnp.bfloat16)
    last_copy = remote(ret2_send, ret2_recv, home_s.at[2], home_r.at[2], peer)
    last_copy.start()
    lax.fori_loop(taken, chunks - 1, line_step, 0)
    mixed_grad[...] += into_tokens(0)
    lax.fori_loop(chunks - 1, chunks, line_step, 0)

    def finish(k, carry):
        total = line_sum(k, layer)
        for step in range(1, depth):
            layer_copy(step, k).wait_recv()
            total = total + z_recv[step - 1, k].astype(jnp.float32)
        factor_ref[k] = total
        return carry

    last_copy.wait_recv()
    grad_ref[...] = (mixed_grad[...] + ret2_recv[...].astype(jnp.float32)).astype(jnp.bfloat16)
    lax.fori_loop(0, chunks, finish, 0)

    fetch_ids.wait_send()
    fetch_x.wait_send()
    home_copy.wait_send()
    pg_copy.wait_send()
    last_copy.wait_send()

    def drain(e, carry):
        core_copy(e).wait_send()
        line_copy(e).wait_send()
        for step in range(1, depth):
            layer_copy(step, e).wait_send()
        return carry

    lax.fori_loop(0, chunks, drain, 0)


def closing_kernel(grad_ref, factor_ref, proj_ref, grad_out, down_grad_out):
    grad_out[...] = grad_ref[...]
    for e in range(down_grad_out.shape[0]):
        turned = jnp.transpose(factor_ref[e])
        high = turned.astype(jnp.bfloat16)
        low = (turned - high.astype(jnp.float32)).astype(jnp.bfloat16)
        down_grad_out[e] = dot_nt(high, proj_ref[...]) + dot_nt(low, proj_ref[...])


def fused(
    hidden_states,
    expert_ids,
    router_weight,
    up_weight,
    down_weight,
    projection,
    teacher_scores,
    query_lengths,
    passage_lengths,
):
    tokens, width = hidden_states.shape
    here, _, units = up_weight.shape
    vec = projection.shape[1]
    queries = teacher_scores.shape[1]
    depth = lax.axis_size("rep") // 4
    rows = 2 * CAP
    parts = 2
    chunks, slab = here * parts, vec // parts
    share = units // lax.axis_size("rep")
    vmem = pl.BlockSpec(memory_space=pltpu.VMEM)
    hbm = pl.BlockSpec(memory_space=pl.ANY)
    half, full = jnp.bfloat16, jnp.float32
    dma = pltpu.SemaphoreType.DMA
    scratch = [
        pltpu.VMEM((here, width, units), half),
        pltpu.VMEM((here, units, width), half),
        pltpu.VMEM((vec, width), full),
        pltpu.VMEM((queries, tokens), full),
        pltpu.VMEM((tokens, width), half),
        pltpu.VMEM((2, tokens), jnp.int32),
        pltpu.VMEM((2, here * CAP, tokens), half),
        pltpu.VMEM((2, tokens, here * CAP), half),
        pltpu.VMEM((here, rows, 1), full),
        pltpu.VMEM((here, rows, width), half),
        pltpu.VMEM((here, rows, units), half),
        pltpu.VMEM((here, rows, units), full),
        pltpu.VMEM((here, CAP, units), full),
        pltpu.VMEM((here, rows, width), full),
        pltpu.VMEM((2, here, CAP, width), half),
        pltpu.VMEM((tokens, vec), full),
        pltpu.VMEM((tokens, vec), half),
        pltpu.VMEM((tokens, vec), half),
        pltpu.VMEM((2, tokens, vec), half),
        pltpu.VMEM((tokens, width), full),
        pltpu.VMEM((here, rows, vec), half),
        pltpu.VMEM((2, here, CAP, width), half),
        pltpu.VMEM((2, E, tokens), full),
        pltpu.VMEM((2, E, tokens), full),
        pltpu.VMEM((2, 1, tokens), full),
        pltpu.VMEM((tokens, width), half),
        pltpu.VMEM((tokens, width), half),
        pltpu.VMEM((2, chunks, 2 * depth, slab, share), half),
        pltpu.VMEM((chunks, 2 * depth, slab, share), half),
        pltpu.VMEM((2, chunks, depth, slab, share), half),
        pltpu.VMEM((chunks, depth, slab, share), half),
        pltpu.VMEM((depth, chunks, slab, share), half),
        pltpu.VMEM((depth - 1, chunks, slab, share), half),
        dma((2, here)),
        dma((2,)),
        dma((2,)),
        dma((3,)),
        dma((3,)),
        dma((chunks,)),
        dma((chunks,)),
        dma((chunks,)),
        dma((chunks,)),
        dma((depth - 1, chunks)),
        dma((depth - 1, chunks)),
    ]
    grad, factor, pair_kl = pl.pallas_call(
        layer_kernel,
        out_shape=(
            jax.ShapeDtypeStruct((tokens, width), half),
            jax.ShapeDtypeStruct((chunks, slab, share), full),
            jax.ShapeDtypeStruct((1, 1), full),
        ),
        in_specs=[vmem, vmem, vmem, hbm, hbm, vmem, vmem, vmem, vmem],
        out_specs=(vmem, vmem, vmem),
        scratch_shapes=scratch,
        compiler_params=pltpu.CompilerParams(
            collective_id=0, has_side_effects=True, vmem_limit_bytes=57 * 1024 * 1024
        ),
    )(
        hidden_states,
        expert_ids.T,
        router_weight.T,
        up_weight,
        down_weight,
        projection,
        teacher_scores[0],
        query_lengths.reshape(1, 1),
        passage_lengths.reshape(1, 1),
    )
    input_grad, down_grad = pl.pallas_call(
        closing_kernel,
        out_shape=(
            jax.ShapeDtypeStruct((tokens, width), half),
            jax.ShapeDtypeStruct((here, share, width), full),
        ),
        in_specs=[vmem, vmem, vmem],
        out_specs=(vmem, vmem),
        compiler_params=pltpu.CompilerParams(vmem_limit_bytes=16 * 1024 * 1024),
    )(grad, factor.reshape(here, vec, share), projection)
    return input_grad, down_grad, pair_kl.reshape(1)


def fits(mesh, hidden_states, up_weight, projection, teacher_scores):
    reps, size = mesh.shape["rep"], mesh.shape["exp"]
    pairs, queries, _ = teacher_scores.shape
    tokens = hidden_states.shape[0] // (reps * size)
    experts, width, units = up_weight.shape
    vec = projection.shape[1]
    return (
        size == 2
        and reps % 4 == 0
        and reps >= 8
        and experts == E
        and pairs == reps * size
        and units == reps * vec
        and vec == 128
        and width % 128 == 0
        and tokens % 128 == 0
        and queries <= 128
        and experts // size >= 2
    )


def solution(mesh):
    placed = (
        P(("rep", "exp"), None),
        P(("rep", "exp"), None),
        P(),
        P("exp", None, None),
        P("exp", None, None),
        P(),
        P(("rep", "exp"), None, None),
        P(("rep", "exp")),
        P(("rep", "exp")),
    )

    def program(*arrays):
        body = fused if fits(mesh, arrays[0], arrays[3], arrays[5], arrays[6]) else local
        return jax.shard_map(
            body,
            mesh=mesh,
            in_specs=placed,
            out_specs=(P(("rep", "exp"), None), P("exp", "rep", None), P(("rep", "exp"))),
            check_vma=False,
        )(*arrays)

    return program
```

```python
import jax
import jax.numpy as jnp
from jax import lax
from jax.experimental import pallas as pl
from jax.experimental.pallas import tpu as pltpu
from jax.sharding import PartitionSpec as P

E = 8
LQ = 32
LP = 224
CAP = 96


score_scale = 20.0
norm_eps = 1e-06
sqrt_half = 0.7071067811865476
density_scale = 0.3989422804014327


def gelu_value(preact):
    return 0.5 * preact * (1.0 + lax.erf(preact * sqrt_half))


def gelu_slope(preact):
    return (
        0.5 * (1.0 + lax.erf(preact * sqrt_half))
        + preact * jnp.exp(-0.5 * preact * preact) * density_scale
    )


def distill(vectors, teacher_scores, query_lengths, passage_lengths):
    queries = vectors[:, :LQ]
    passages = vectors[:, LQ:]
    scores = score_scale * jnp.einsum(
        "pqv,pkv->pqk", queries, passages, precision=lax.Precision.HIGHEST
    )
    query_mask = (jnp.arange(LQ, dtype=jnp.int32)[None, :] < query_lengths[:, None]).astype(
        jnp.float32
    )
    passage_mask = (jnp.arange(LP, dtype=jnp.int32)[None, :] < passage_lengths[:, None]).astype(
        jnp.float32
    )
    student_exp = jnp.exp(scores) * passage_mask[:, None, :]
    student_total = jnp.sum(student_exp, axis=-1, keepdims=True)
    student = student_exp / student_total
    log_student = scores - jnp.log(student_total)
    teacher_exp = jnp.exp(teacher_scores) * passage_mask[:, None, :]
    teacher_total = jnp.sum(teacher_exp, axis=-1, keepdims=True)
    teacher = teacher_exp / teacher_total
    log_teacher = teacher_scores - jnp.log(teacher_total)
    per_query = jnp.sum(teacher * (log_teacher - log_student), axis=-1)
    pair_kl = jnp.sum(per_query * query_mask, axis=-1)
    score_grad = (student - teacher) * query_mask[:, :, None]
    query_grad = score_scale * jnp.einsum(
        "pqk,pkv->pqv", score_grad, passages, precision=lax.Precision.HIGHEST
    )
    passage_grad = score_scale * jnp.einsum(
        "pqk,pqv->pkv", score_grad, queries, precision=lax.Precision.HIGHEST
    )
    return (pair_kl, jnp.concatenate([query_grad, passage_grad], axis=1))


def fetch(block, shift):
    size = lax.axis_size("exp")
    return lax.ppermute(block, "exp", [(i, (i - shift) % size) for i in range(size)])


def give_back(block, shift):
    size = lax.axis_size("exp")
    return lax.ppermute(block, "exp", [(i, (i + shift) % size) for i in range(size)])


def spread_out(block):
    size = lax.axis_size("exp")
    return jnp.stack([block] + [fetch(block, shift) for shift in range(1, size)])


def bring_home(parts):
    total = parts[0]
    for shift in range(1, parts.shape[0]):
        total = total + give_back(parts[shift].astype(jnp.bfloat16), shift).astype(jnp.float32)
    return total


def halving_orders(bits, experts):
    near = list(range(bits))
    late = [0] + list(range(2, bits)) + [1] if bits > 2 else near
    return [late if expert % 4 == 3 else near for expert in range(experts)]


def weight_grad(hidden, gated, projection, gate_rows):
    size = lax.axis_size("rep")
    bits = size.bit_length() - 1
    experts, _, units = hidden.shape
    width = gated.shape[-1]
    share = units // size
    index = lax.axis_index("rep")
    product = jnp.einsum(
        "erf,erv->efv", hidden, gated, preferred_element_type=jnp.float32
    ).astype(jnp.bfloat16)

    def swap(block, bit):
        return lax.ppermute(block, "rep", [(i, i ^ (1 << bit)) for i in range(size)])

    orders = halving_orders(bits, experts)
    left = [list(range(bits - 1, -1, -1)) for _ in range(experts)]
    held = [[product[e]] for e in range(experts)]
    for step in range(bits):
        sent = []
        for e in range(experts):
            bit = orders[e][step]
            axis = left[e].index(bit)
            shape = (2,) * len(left[e]) + (share, width)
            here = (index >> bit) % 2

            def half(side):
                total = None
                for term in held[e]:
                    piece = lax.dynamic_index_in_dim(
                        term.reshape(shape), side, axis=axis, keepdims=False
                    ).astype(jnp.float32)
                    total = piece if total is None else total + piece
                return total

            sent.append(half(1 - here).astype(jnp.bfloat16))
            held[e] = [half(here)]
            left[e].remove(bit)
        for e in range(experts):
            held[e].append(swap(sent[e], orders[e][step]))
        if step == min(1, bits - 1):
            held[-1], gate_rows = lax.optimization_barrier((held[-1], gate_rows))
    shares = [
        sum(term.astype(jnp.float32).reshape(share, width) for term in held[e])
        for e in range(experts)
    ]
    factor = jnp.stack(shares)
    grad = jnp.einsum(
        "efv,dv->efd",
        factor,
        projection.astype(jnp.float32),
        precision=lax.Precision.HIGHEST,
    )
    return grad, gate_rows


def local(
    hidden_states,
    expert_ids,
    router_weight,
    up_weight,
    down_weight,
    projection,
    teacher_scores,
    query_lengths,
    passage_lengths,
):
    tok_rows, width = hidden_states.shape
    here = up_weight.shape[0]
    first = lax.axis_index("exp") * here
    rows = spread_out(hidden_states)
    ids = spread_out(expert_ids.T)
    blocks = rows.shape[0]
    names = jnp.arange(E, dtype=jnp.int32)[None, :, None]
    is_first = (ids[:, :1] == names).astype(jnp.float32)
    is_second = (ids[:, 1:] == names).astype(jnp.float32)
    logits = jnp.einsum("de,ntd->net", router_weight, rows, preferred_element_type=jnp.float32)
    side = is_first - is_second
    first_gate = jax.nn.sigmoid(jnp.sum(logits * side, axis=1, keepdims=True))
    second_gate = 1.0 - first_gate
    named = is_first + is_second
    before = jnp.arange(tok_rows)[:, None] < jnp.arange(tok_rows)[None, :]
    slots = jnp.einsum(
        "net,tu->neu",
        named.astype(jnp.bfloat16),
        before.astype(jnp.bfloat16),
        preferred_element_type=jnp.float32,
    ).astype(jnp.int32)
    slots = jnp.where(named > 0, slots, -1)
    mine = lambda value: lax.dynamic_slice_in_dim(value, first, here, axis=1)
    slots_here = mine(slots)
    gates_here = mine(is_first * first_gate + is_second * second_gate)
    side_here = mine(side)
    hit = slots_here[:, :, None, :] == jnp.arange(CAP, dtype=jnp.int32)[None, None, :, None]
    pick = hit.astype(jnp.bfloat16)
    row_gate = jnp.sum(jnp.where(hit, gates_here[:, :, None, :], 0.0), axis=-1)
    row_gate = row_gate.transpose(1, 0, 2).reshape(here, blocks * CAP, 1)

    def to_slots(tokens):
        picked = jnp.einsum("nect,ntd->encd", pick, tokens, preferred_element_type=jnp.float32)
        return picked.astype(jnp.bfloat16).reshape(here, blocks * CAP, -1)

    def to_tokens(slot_rows):
        return jnp.einsum(
            "nect,encd->ntd",
            pick,
            slot_rows.reshape(here, blocks, CAP, width),
            preferred_element_type=jnp.float32,
        )

    expert_rows = to_slots(rows)
    preact = jnp.einsum(
        "erd,edf->erf", expert_rows, up_weight, preferred_element_type=jnp.float32
    )
    hidden = gelu_value(preact).astype(jnp.bfloat16)
    out = jnp.einsum("erf,efd->erd", hidden, down_weight, preferred_element_type=jnp.float32)
    mixed = bring_home(to_tokens((row_gate * out).astype(jnp.bfloat16)))
    mixed_rows = (hidden_states.astype(jnp.float32) + mixed).astype(jnp.bfloat16)
    projected = jnp.dot(mixed_rows, projection, preferred_element_type=jnp.float32)
    vec_norm = jnp.sqrt(jnp.sum(projected * projected, axis=-1, keepdims=True) + norm_eps)
    vectors = projected / vec_norm
    pairs_here = teacher_scores.shape[0]
    pair_kl, vector_grad = distill(
        vectors.reshape(pairs_here, -1, projected.shape[1]),
        teacher_scores,
        query_lengths,
        passage_lengths,
    )
    vector_grad = vector_grad.reshape(tok_rows, -1)
    radial = jnp.sum(vectors * vector_grad, axis=-1, keepdims=True)
    projected_grad = ((vector_grad - vectors * radial) / vec_norm).astype(jnp.bfloat16)
    mixed_grad = jnp.dot(projected_grad, projection.T, preferred_element_type=jnp.float32)
    pg_rows = to_slots(spread_out(projected_grad))
    grad_rows = jnp.einsum(
        "erv,dv->erd", pg_rows, projection, preferred_element_type=jnp.float32
    )
    out_grad = (row_gate * grad_rows).astype(jnp.bfloat16)
    gated = (row_gate * pg_rows.astype(jnp.float32)).astype(jnp.bfloat16)
    down_grad, out_grad = weight_grad(hidden, gated, projection, out_grad)
    gate_grad = jnp.sum(grad_rows * out, axis=-1).reshape(here, blocks, CAP).transpose(1, 0, 2)
    hit_grad = jnp.sum(jnp.where(hit, gate_grad[..., None], 0.0), axis=2)
    spread = jnp.sum(hit_grad * side_here, axis=1, keepdims=True) * first_gate * second_gate
    router_part = jnp.einsum(
        "net,de->ntd",
        spread * side,
        router_weight.astype(jnp.float32),
        precision=lax.Precision.HIGHEST,
    )
    hidden_grad = jnp.einsum(
        "erd,efd->erf", out_grad, down_weight, preferred_element_type=jnp.float32
    )
    pre_grad = (hidden_grad * gelu_slope(preact)).astype(jnp.bfloat16)
    row_grad = jnp.einsum(
        "erf,edf->erd", pre_grad, up_weight, preferred_element_type=jnp.float32
    ).astype(jnp.bfloat16)
    input_grad = (mixed_grad + bring_home(to_tokens(row_grad) + router_part)).astype(jnp.bfloat16)
    return (input_grad, down_grad, pair_kl)


def tall(value, rows):
    return jnp.concatenate(
        [value, jnp.zeros((rows - value.shape[0], value.shape[1]), value.dtype)], axis=0
    )


def dot_nn(left, right, precision=None):
    return lax.dot_general(
        left,
        right,
        (((1,), (0,)), ((), ())),
        precision=precision,
        preferred_element_type=jnp.float32,
    )


def dot_nt(left, right, precision=None):
    return lax.dot_general(
        left,
        right,
        (((1,), (1,)), ((), ())),
        precision=precision,
        preferred_element_type=jnp.float32,
    )


def layer_kernel(
    x_hbm,
    ids_hbm,
    rw_hbm,
    up_hbm,
    down_hbm,
    proj_hbm,
    teacher_hbm,
    qlen_ref,
    plen_ref,
    grad_ref,
    factor_ref,
    kl_ref,
    x_ref,
    ids_ref,
    rw_ref,
    proj_ref,
    teacher_ref,
    up_v,
    down_v,
    rwp,
    tpad,
    px,
    pids,
    pick,
    spread_pick,
    row_gate,
    rows_ref,
    hid,
    slope,
    held,
    out_ref,
    gated_out,
    home,
    ret_send,
    ret_recv,
    pg,
    mixed_grad,
    pg_rows,
    back,
    coef,
    hitg,
    logit_hits,
    ret2_send,
    ret2_recv,
    core_send,
    core_recv,
    x_send,
    x_recv,
    z_send,
    z_recv,
    weight_sem,
    input_sem,
    fetch_s,
    fetch_r,
    home_s,
    home_r,
    core_s,
    core_r,
    x_s,
    x_r,
    z_s,
    z_r,
):
    tokens, width = x_ref.shape
    here, _, units = up_v.shape
    vec = proj_ref.shape[1]
    lanes = vec
    queries = teacher_ref.shape[0]
    size = lax.axis_size("exp")
    reps = lax.axis_size("rep")
    depth = reps // 4
    rep = lax.axis_index("rep")
    own = lax.axis_index("exp")
    core, line, layer = rep % 2, (rep // 2) % 2, rep // 4
    share = units // reps
    wide = 2 * lanes
    tiles = units // wide

    peer = {"exp": 1 - own}
    core_peer = {"rep": rep + 1 - 2 * core}
    line_peer = {"rep": rep + 2 - 4 * line}

    def layer_peer(step):
        return {"rep": ((layer + step) % depth) * 4 + rep % 4}

    def remote(src, dst, send, recv, device):
        return pltpu.make_async_remote_copy(
            src_ref=src,
            dst_ref=dst,
            send_sem=send,
            recv_sem=recv,
            device_id=device,
            device_id_type=pl.DeviceIdType.MESH,
        )

    def up_copy(e):
        return pltpu.make_async_copy(up_hbm.at[e], up_v.at[e], weight_sem.at[0, e])

    def down_copy(e):
        return pltpu.make_async_copy(down_hbm.at[e], down_v.at[e], weight_sem.at[1, e])

    barrier = pltpu.get_barrier_semaphore()
    for device in [peer, core_peer, line_peer] + [layer_peer(k) for k in range(1, depth)]:
        pl.semaphore_signal(
            barrier, inc=1, device_id=device, device_id_type=pl.DeviceIdType.MESH
        )
    inputs = [
        pltpu.make_async_copy(source, target, input_sem.at[k])
        for k, (source, target) in enumerate(
            [
                (ids_hbm, ids_ref),
                (rw_hbm, rw_ref),
                (x_hbm, x_ref),
                (proj_hbm, proj_ref),
                (teacher_hbm, teacher_ref),
            ]
        )
    ]
    for copy in inputs:
        copy.start()
    for e in range(here):
        up_copy(e).start()
    for e in range(here):
        down_copy(e).start()
    pl.semaphore_wait(barrier, 2 + depth)

    fetch_x = remote(x_hbm, px, fetch_s.at[0], fetch_r.at[0], peer)
    fetch_ids = remote(ids_hbm, pids, fetch_s.at[1], fetch_r.at[1], peer)
    fetch_ids.start()
    fetch_x.start()
    for copy in inputs:
        copy.wait()

    rwp[...] = tall(rw_ref[...].astype(jnp.float32), lanes)
    earlier = lax.broadcasted_iota(jnp.int32, (tokens, tokens), 0)
    later = lax.broadcasted_iota(jnp.int32, (tokens, tokens), 1)
    before = jnp.where(earlier < later, 1.0, 0.0).astype(jnp.bfloat16)

    def mine(value):
        picked = value
        for side in range(1, size):
            moved = pltpu.roll(value, (E - side * here) % E, 0)
            picked = jnp.where(own == side, moved, picked)
        return picked

    def prepare(n, ids, tokens_rows):
        names = lax.broadcasted_iota(jnp.int32, (E, tokens), 0)
        is_first = jnp.where(ids[0:1] == names, 1.0, 0.0)
        is_second = jnp.where(ids[1:2] == names, 1.0, 0.0)
        logits = dot_nt(rw_ref[...], tokens_rows)
        side = is_first - is_second
        first_gate = jax.nn.sigmoid(jnp.sum(logits * side, axis=0, keepdims=True))
        second_gate = 1.0 - first_gate
        named = is_first + is_second
        slots = dot_nn(named.astype(jnp.bfloat16), before)
        slots = mine(jnp.where(named > 0, slots, -1.0))
        gates = mine(is_first * first_gate + is_second * second_gate)
        coef[n] = side * (first_gate * second_gate)
        hitg[n] = mine(side)
        place = lax.broadcasted_iota(jnp.int32, (CAP, tokens), 0).astype(jnp.float32)
        for e in range(here):
            hit = slots[e : e + 1] == place
            pick[n, e * CAP : (e + 1) * CAP, :] = jnp.where(hit, 1.0, 0.0).astype(jnp.bfloat16)
            row_gate[e, n * CAP : (n + 1) * CAP, :] = jnp.sum(
                jnp.where(hit, gates[e : e + 1], 0.0), axis=1, keepdims=True
            )
        by_token = jnp.transpose(tall(slots, lanes))
        column = lax.broadcasted_iota(jnp.int32, (tokens, here * CAP), 1)
        want = column
        have = jnp.broadcast_to(by_token[:, 0:1], column.shape)
        for e in range(1, here):
            inside = column >= e * CAP
            have = jnp.where(inside, by_token[:, e : e + 1], have)
            want = jnp.where(inside, column - e * CAP, want)
        spread_pick[n] = jnp.where(have == want.astype(jnp.float32), 1.0, 0.0).astype(
            jnp.bfloat16
        )
        gathered = dot_nn(pick[n], tokens_rows).astype(jnp.bfloat16)
        for e in range(here):
            rows_ref[e, n * CAP : (n + 1) * CAP, :] = gathered[e * CAP : (e + 1) * CAP]

    def density(preact):
        return preact * jnp.exp(-0.5 * preact * preact) * density_scale

    def rise(n, e):
        block = rows_ref[e, n * CAP : (n + 1) * CAP, :]
        for j in range(tiles):
            cut = slice(j * wide, (j + 1) * wide)
            preact = dot_nn(block, up_v[e, :, cut])
            half = 0.5 * (1.0 + lax.erf(preact * sqrt_half))
            hid[e, n * CAP : (n + 1) * CAP, cut] = (preact * half).astype(jnp.bfloat16)
            if n == 0:
                half = half + density(preact)
            else:
                held[e, :, cut] = preact
            slope[e, n * CAP : (n + 1) * CAP, cut] = half

    prepare(0, ids_ref[...], x_ref[...])

    def first_pass(e, carry):
        up_copy(e).wait()
        rise(0, e)
        return carry

    lax.fori_loop(0, here, first_pass, 0)
    fetch_ids.wait_recv()
    fetch_x.wait_recv()
    prepare(1, pids[...], px[...])

    def sink(e):
        out = dot_nn(hid[e], down_v[e])
        out_ref[e] = out
        gated = (row_gate[e] * out).astype(jnp.bfloat16)
        gated_out[0, e] = gated[0:CAP]
        gated_out[1, e] = gated[CAP:]

    for e in range(here):
        down_copy(e).wait()
    rise(1, 0)
    for e in range(1, here):
        rise(1, e)
        sink(e - 1)
    sink(here - 1)
    def to_vectors(n):
        rows = dot_nn(gated_out[n].reshape(here * CAP, width), proj_ref[...])
        return dot_nn(spread_pick[n], rows.astype(jnp.bfloat16))

    ret_send[...] = to_vectors(1).astype(jnp.bfloat16)
    home_copy = remote(ret_send, ret_recv, home_s.at[0], home_r.at[0], peer)
    home_copy.start()
    home[...] = dot_nn(x_ref[...], proj_ref[...]) + to_vectors(0)

    def steepen(e, carry):
        for j in range(tiles):
            cut = slice(j * wide, (j + 1) * wide)
            slope[e, CAP:, cut] += density(held[e, :, cut])
        return carry

    lax.fori_loop(0, here, steepen, 0)
    keys = lax.broadcasted_iota(jnp.int32, (queries, tokens), 1) - queries
    valid = jnp.where((keys >= 0) & (keys < plen_ref[...]), 1.0, 0.0)
    asked = jnp.where(
        lax.broadcasted_iota(jnp.int32, (queries, 1), 0) < qlen_ref[...], 1.0, 0.0
    )
    tpad[...] = jnp.zeros_like(tpad)
    tpad[:, 0 : tokens - queries] = teacher_ref[...]
    teacher_scores = pltpu.roll(tpad[...], queries, 1)
    teacher_exp = jnp.exp(teacher_scores) * valid
    teacher_total = jnp.sum(teacher_exp, axis=1, keepdims=True)
    teacher = teacher_exp / teacher_total
    log_teacher = teacher_scores - jnp.log(teacher_total)
    home_copy.wait_recv()
    projected = home[...] + ret_recv[...].astype(jnp.float32)
    vec_norm = jnp.sqrt(jnp.sum(projected * projected, axis=1, keepdims=True) + norm_eps)
    vectors = projected / vec_norm
    best = lax.Precision.HIGHEST
    scores = score_scale * dot_nt(vectors[0:queries], vectors, best)
    student_exp = jnp.exp(scores) * valid
    student_total = jnp.sum(student_exp, axis=1, keepdims=True)
    student = student_exp / student_total
    log_student = scores - jnp.log(student_total)
    per_query = jnp.sum(teacher * (log_teacher - log_student), axis=1, keepdims=True)
    kl_ref[...] = jnp.sum(per_query * asked, axis=0, keepdims=True)
    score_grad = (student - teacher) * asked
    query_grad = dot_nn(score_grad, vectors, best)
    passage_grad = dot_nn(jnp.transpose(tall(score_grad, lanes)), vectors[0:lanes], best)
    vector_grad = score_scale * (passage_grad + tall(query_grad, tokens))
    radial = jnp.sum(vectors * vector_grad, axis=1, keepdims=True)
    pg[0] = ((vector_grad - vectors * radial) / vec_norm).astype(jnp.bfloat16)
    pg_copy = remote(pg.at[0], pg.at[1], home_s.at[1], home_r.at[1], peer)
    pg_copy.start()

    def take_rows(n):
        picked = dot_nn(pick[n], pg[n]).astype(jnp.bfloat16)
        for e in range(here):
            pg_rows[e, n * CAP : (n + 1) * CAP, :] = picked[e * CAP : (e + 1) * CAP]

    take_rows(0)
    mixed_grad[...] = dot_nt(pg[0], proj_ref[...])
    pg_copy.wait_recv()
    take_rows(1)

    parts = core_send.shape[1] // here
    chunks = here * parts
    slab = vec // parts

    def core_copy(e):
        return remote(
            core_send.at[1 - core, e], core_recv.at[e], core_s.at[e], core_r.at[e], core_peer
        )

    def line_copy(e):
        return remote(x_send.at[1 - line, e], x_recv.at[e], x_s.at[e], x_r.at[e], line_peer)

    def layer_copy(step, e):
        return remote(
            z_send.at[(layer + step) % depth, e],
            z_recv.at[step - 1, e],
            z_s.at[step - 1, e],
            z_r.at[step - 1, e],
            layer_peer(step),
        )

    def factor(e, carry):
        gated = row_gate[e] * pg_rows[e].astype(jnp.float32)
        turned = jnp.transpose(gated).astype(jnp.bfloat16)
        product = dot_nn(turned, hid[e]).astype(jnp.bfloat16)
        for p in range(parts):
            for r in range(reps):
                core_send[r % 2, e * parts + p, r // 2] = product[
                    p * slab : (p + 1) * slab, r * share : (r + 1) * share
                ]
            core_copy(e * parts + p).start()

        @pl.when(e >= 1)
        def _():
            for p in range(parts):
                after_core((e - 1) * parts + p)

        return carry

    def after_core(e):
        core_copy(e).wait_recv()
        for k in range(2 * depth):
            total = core_send[core, e, k].astype(jnp.float32) + core_recv[e, k].astype(
                jnp.float32
            )
            x_send[k % 2, e, k // 2] = total.astype(jnp.bfloat16)
        line_copy(e).start()

    lax.fori_loop(0, here, factor, 0)
    for p in range(parts):
        after_core((here - 1) * parts + p)

    def line_sum(e, k):
        return x_send[line, e, k].astype(jnp.float32) + x_recv[e, k].astype(jnp.float32)

    def after_line(e):
        line_copy(e).wait_recv()
        for k in range(depth):
            z_send[k, e] = line_sum(e, k).astype(jnp.bfloat16)
        for step in range(1, depth):
            layer_copy(step, e).start()

    def fall(e, carry):
        upstream = dot_nt(pg_rows[e], proj_ref[...])
        grad = jnp.sum(upstream * out_ref[e], axis=1, keepdims=True)
        place = lax.broadcasted_iota(jnp.int32, (CAP, tokens), 0).astype(jnp.float32)
        for n in range(2):
            hits = jnp.sum(
                pick[n, pl.ds(pl.multiple_of(e * CAP, CAP), CAP), :].astype(jnp.float32)
                * grad[n * CAP : (n + 1) * CAP],
                axis=0,
                keepdims=True,
            )
            logit_hits[n] += hits * hitg[n, pl.ds(e, 1), :]
        out_grad = (row_gate[e] * upstream).astype(jnp.bfloat16)
        total = None
        for j in range(tiles):
            cut = slice(j * wide, (j + 1) * wide)
            hidden_grad = dot_nt(out_grad, down_v[e, cut, :])
            pre_grad = (hidden_grad * slope[e, :, cut]).astype(jnp.bfloat16)
            part = dot_nt(pre_grad, up_v[e, :, cut])
            total = part if total is None else total + part
        rounded = total.astype(jnp.bfloat16)
        back[0, e] = rounded[0:CAP]
        back[1, e] = rounded[CAP:]

        lax.fori_loop(e * taken // here, (e + 1) * taken // here, line_step, 0)
        return carry

    taken = max(chunks - 2, 1)

    def line_step(k, carry):
        after_line(k)
        return carry

    logit_hits[...] = jnp.zeros_like(logit_hits)
    lax.fori_loop(0, here, fall, 0)

    def into_tokens(n):
        logit_grad = jnp.transpose(tall(logit_hits[n] * coef[n], lanes))
        return dot_nn(spread_pick[n], back[n].reshape(here * CAP, width)) + dot_nn(
            logit_grad, rwp[...], best
        )

    ret2_send[...] = into_tokens(1).astype(jnp.bfloat16)
    last_copy = remote(ret2_send, ret2_recv, home_s.at[2], home_r.at[2], peer)
    last_copy.start()
    lax.fori_loop(taken, chunks - 1, line_step, 0)
    mixed_grad[...] += into_tokens(0)
    lax.fori_loop(chunks - 1, chunks, line_step, 0)

    def finish(k, carry):
        total = line_sum(k, layer)
        for step in range(1, depth):
            layer_copy(step, k).wait_recv()
            total = total + z_recv[step - 1, k].astype(jnp.float32)
        factor_ref[k] = total
        return carry

    last_copy.wait_recv()
    grad_ref[...] = (mixed_grad[...] + ret2_recv[...].astype(jnp.float32)).astype(jnp.bfloat16)
    lax.fori_loop(0, chunks, finish, 0)

    fetch_ids.wait_send()
    fetch_x.wait_send()
    home_copy.wait_send()
    pg_copy.wait_send()
    last_copy.wait_send()

    def drain(e, carry):
        core_copy(e).wait_send()
        line_copy(e).wait_send()
        for step in range(1, depth):
            layer_copy(step, e).wait_send()
        return carry

    lax.fori_loop(0, chunks, drain, 0)


def closing_kernel(grad_ref, factor_ref, proj_ref, grad_out, down_grad_out):
    grad_out[...] = grad_ref[...]
    for e in range(down_grad_out.shape[0]):
        turned = jnp.transpose(factor_ref[e])
        high = turned.astype(jnp.bfloat16)
        low = (turned - high.astype(jnp.float32)).astype(jnp.bfloat16)
        down_grad_out[e] = dot_nt(high, proj_ref[...]) + dot_nt(low, proj_ref[...])


def fused(
    hidden_states,
    expert_ids,
    router_weight,
    up_weight,
    down_weight,
    projection,
    teacher_scores,
    query_lengths,
    passage_lengths,
):
    tokens, width = hidden_states.shape
    here, _, units = up_weight.shape
    vec = projection.shape[1]
    queries = teacher_scores.shape[1]
    depth = lax.axis_size("rep") // 4
    rows = 2 * CAP
    parts = 2
    chunks, slab = here * parts, vec // parts
    share = units // lax.axis_size("rep")
    vmem = pl.BlockSpec(memory_space=pltpu.VMEM)
    hbm = pl.BlockSpec(memory_space=pltpu.HBM)
    half, full = jnp.bfloat16, jnp.float32
    dma = pltpu.SemaphoreType.DMA
    scratch = [
        pltpu.VMEM((tokens, width), half),
        pltpu.VMEM((2, tokens), jnp.int32),
        pltpu.VMEM((E, width), half),
        pltpu.VMEM((width, vec), half),
        pltpu.VMEM(teacher_scores.shape[1:], full),
        pltpu.VMEM((here, width, units), half),
        pltpu.VMEM((here, units, width), half),
        pltpu.VMEM((vec, width), full),
        pltpu.VMEM((queries, tokens), full),
        pltpu.VMEM((tokens, width), half),
        pltpu.VMEM((2, tokens), jnp.int32),
        pltpu.VMEM((2, here * CAP, tokens), half),
        pltpu.VMEM((2, tokens, here * CAP), half),
        pltpu.VMEM((here, rows, 1), full),
        pltpu.VMEM((here, rows, width), half),
        pltpu.VMEM((here, rows, units), half),
        pltpu.VMEM((here, rows, units), full),
        pltpu.VMEM((here, CAP, units), full),
        pltpu.VMEM((here, rows, width), full),
        pltpu.VMEM((2, here, CAP, width), half),
        pltpu.VMEM((tokens, vec), full),
        pltpu.VMEM((tokens, vec), half),
        pltpu.VMEM((tokens, vec), half),
        pltpu.VMEM((2, tokens, vec), half),
        pltpu.VMEM((tokens, width), full),
        pltpu.VMEM((here, rows, vec), half),
        pltpu.VMEM((2, here, CAP, width), half),
        pltpu.VMEM((2, E, tokens), full),
        pltpu.VMEM((2, E, tokens), full),
        pltpu.VMEM((2, 1, tokens), full),
        pltpu.VMEM((tokens, width), half),
        pltpu.VMEM((tokens, width), half),
        pltpu.VMEM((2, chunks, 2 * depth, slab, share), half),
        pltpu.VMEM((chunks, 2 * depth, slab, share), half),
        pltpu.VMEM((2, chunks, depth, slab, share), half),
        pltpu.VMEM((chunks, depth, slab, share), half),
        pltpu.VMEM((depth, chunks, slab, share), half),
        pltpu.VMEM((depth - 1, chunks, slab, share), half),
        dma((2, here)),
        dma((5,)),
        dma((2,)),
        dma((2,)),
        dma((3,)),
        dma((3,)),
        dma((chunks,)),
        dma((chunks,)),
        dma((chunks,)),
        dma((chunks,)),
        dma((depth - 1, chunks)),
        dma((depth - 1, chunks)),
    ]
    grad, factor, pair_kl = pl.pallas_call(
        layer_kernel,
        out_shape=(
            jax.ShapeDtypeStruct((tokens, width), half),
            jax.ShapeDtypeStruct((chunks, slab, share), full),
            jax.ShapeDtypeStruct((1, 1), full),
        ),
        in_specs=[hbm] * 7 + [vmem] * 2,
        out_specs=(vmem, vmem, vmem),
        scratch_shapes=scratch,
        compiler_params=pltpu.CompilerParams(
            collective_id=0, has_side_effects=True, vmem_limit_bytes=57 * 1024 * 1024
        ),
    )(
        hidden_states,
        expert_ids.T,
        router_weight.T,
        up_weight,
        down_weight,
        projection,
        teacher_scores[0],
        query_lengths.reshape(1, 1),
        passage_lengths.reshape(1, 1),
    )
    input_grad, down_grad = pl.pallas_call(
        closing_kernel,
        out_shape=(
            jax.ShapeDtypeStruct((tokens, width), half),
            jax.ShapeDtypeStruct((here, share, width), full),
        ),
        in_specs=[vmem, vmem, vmem],
        out_specs=(vmem, vmem),
        compiler_params=pltpu.CompilerParams(vmem_limit_bytes=57 * 1024 * 1024),
    )(grad, factor.reshape(here, vec, share), projection)
    return input_grad, down_grad, pair_kl.reshape(1)


def fits(mesh, hidden_states, up_weight, projection, teacher_scores):
    reps, size = mesh.shape["rep"], mesh.shape["exp"]
    pairs, queries, _ = teacher_scores.shape
    tokens = hidden_states.shape[0] // (reps * size)
    experts, width, units = up_weight.shape
    vec = projection.shape[1]
    return (
        size == 2
        and reps % 4 == 0
        and reps >= 8
        and experts == E
        and pairs == reps * size
        and units == reps * vec
        and vec == 128
        and width % 128 == 0
        and tokens % 128 == 0
        and queries <= 128
        and experts // size >= 2
    )


def solution(mesh):
    placed = (
        P(("rep", "exp"), None),
        P(("rep", "exp"), None),
        P(),
        P("exp", None, None),
        P("exp", None, None),
        P(),
        P(("rep", "exp"), None, None),
        P(("rep", "exp")),
        P(("rep", "exp")),
    )

    def program(*arrays):
        body = fused if fits(mesh, arrays[0], arrays[3], arrays[5], arrays[6]) else local
        return jax.shard_map(
            body,
            mesh=mesh,
            in_specs=placed,
            out_specs=(P(("rep", "exp"), None), P("exp", "rep", None), P(("rep", "exp"))),
            check_vma=False,
        )(*arrays)

    return program
```
